32 devices in a mesh: chan: 8 (over y, x, core), seq: 4 (over z).
Axes of the slice: x: 2, y: 2, z: 4, core: 2. Of those that a mesh axis runs over, the one named last changes fastest.
Arguments:
- value: bfloat16 [8, 128, 32768], P('seq', 'chan'), may hold values from -6 to 6
- gate_in: bfloat16 [8, 128, 32768], P('seq', 'chan'), may hold values from -6 to 6
- gate_out: bfloat16 [8, 128, 32768], P('seq', 'chan'), may hold values from -6 to 6
- cotangent: bfloat16 [8, 128, 32768], P('seq', 'chan'), may hold values from -6 to 6
- skip_gain: float32 [128], P('chan'), may hold values from 0.25 to 1.5
- weight_in: float32 [64, 33], replicated, may hold values from -1 to 1
- bias_in: float32 [64], replicated, may hold values from -1 to 1
- weight_mid: float32 [2, 64, 64], replicated, may hold values from -0.75 to 0.75
- bias_mid: float32 [2, 64], replicated, may hold values from -1 to 1
- weight_out: float32 [128, 64], replicated, may hold values from -0.75 to 0.75
- decay_rate: float32 [128], replicated, may hold values from 3 to 15
Outputs:
- grad_value: bfloat16 [8, 128, 32768], P('seq', 'chan')
- grad_gate_in: bfloat16 [8, 128, 32768], P('seq', 'chan')
- grad_gate_out: bfloat16 [8, 128, 32768], P('seq', 'chan')
- grad_skip: float32 [128], P('chan')
- grad_weight_in: float32 [64, 33], replicated
- grad_bias_in: float32 [64], replicated
- grad_weight_mid: float32 [2, 64, 64], replicated
- grad_bias_mid: float32 [2, 64], replicated
- grad_weight_out: float32 [128, 64], replicated
- grad_rate: float32 [128], replicated
The draws below stay inside these ranges and needn't reach their ends.
All inputs are finite; a program needn't handle non-finite values.
Results may differ from the reference program's by a relative error of at most 0.009.
Values sent between devices are 32-bit elements; how exact they have to be, the bound alone decides.
No kernel may reach another device: no remote copies, remote signals or barrier semaphores. Data moves between devices by JAX's collectives and lax.ppermute only.
A program may use at most 192 MiB of HBM per device.

```python
import math
import jax
import jax.numpy as jnp
import numpy as np
from jax import lax

L = 32768
CH = 128
ORDER = 64
EMB = 33
BATCH = 8


def levels(key, shape, split, least, largest):
    level = 1.0
    for dim, parts in split:
        heights = jax.random.uniform(jax.random.fold_in(jax.random.fold_in(key, 6), dim), (parts,), jnp.float32, least / len(split), largest / len(split))
        level = level * jnp.repeat(jnp.exp(heights), shape[dim] // parts).reshape((-1,) + (1,) * (len(shape) - 1 - dim))
    return level


def centred(rng, extent, scale, reach, shards=(), kind=jnp.bfloat16):
    loudness = levels(rng, extent, shards, -0.22, 0.18) if shards else 1.0
    entries = jax.random.normal(rng, extent, jnp.float32) * scale * loudness
    return jnp.minimum(jnp.maximum(entries, -reach), reach).astype(kind)


def setup_inputs(seed: int = 0) -> dict:
    key_of = jax.random.split(jax.random.key(seed), 12)
    return {
        "value": centred(key_of[0], (BATCH, CH, L), 1.0, 6.0, ((0, 4), (1, 8))),
        "gate_in": centred(key_of[1], (BATCH, CH, L), 1.0, 6.0, ((0, 4), (1, 8))),
        "gate_out": centred(key_of[2], (BATCH, CH, L), 1.0, 6.0, ((0, 4), (1, 8))),
        "cotangent": centred(key_of[3], (BATCH, CH, L), 1.0, 6.0, ((0, 4), (1, 8))),
        "skip_gain": jnp.clip(0.25 + 1.25 * jax.random.uniform(key_of[4], (CH,), jnp.float32) ** levels(key_of[4], (CH,), ((0, 8),), -0.2, 0.2), 0.25, 1.5),
        "weight_in": centred(key_of[5], (ORDER, EMB), EMB ** -0.5, 1.0, (), jnp.float32),
        "bias_in": jnp.clip(jax.random.uniform(key_of[6], (ORDER,), jnp.float32, -1.0, 1.0), -1.0, 1.0),
        "weight_mid": centred(key_of[7], (2, ORDER, ORDER), ORDER ** -0.5, 0.75, (), jnp.float32),
        "bias_mid": jnp.clip(jax.random.uniform(key_of[8], (2, ORDER), jnp.float32, -1.0, 1.0), -1.0, 1.0),
        "weight_out": centred(key_of[9], (CH, ORDER), ORDER ** -0.5, 0.75, (), jnp.float32),
        "decay_rate": jnp.clip(jnp.exp(jax.random.uniform(key_of[10], (CH,), jnp.float32, math.log(3.0), math.log(15.0))), 3.0, 15.0),
    }


EPSILON = 1e-06
HIGHEST = lax.Precision.HIGHEST

def band_table(length, bands):
    highest = length / 4.0
    return np.array([math.floor(highest ** (number / (bands - 1)) + 0.5) for number in range(bands)], np.int32)

def embedding(positions, length, bands):
    band_freq = jnp.asarray(band_table(length, bands)).astype(jnp.int32)
    phase = positions[None, :] * band_freq[:, None] % length
    angle = 2.0 * math.pi / length * phase.astype(jnp.float32)
    linear = (positions.astype(jnp.float32) / length)[None, :]
    return jnp.concatenate([linear, jnp.cos(angle), jnp.sin(angle)], axis=0)

def filter_rows(weight_in, bias_in, weight_mid, bias_mid, weight_out, decay_rate, positions, length):
    bands = (weight_in.shape[1] - 1) // 2
    feature = embedding(positions, length, bands)
    hidden = jnp.sin(jnp.dot(weight_in, feature, precision=HIGHEST) + bias_in[:, None])
    for middle in range(2):
        hidden = jnp.sin(jnp.dot(weight_mid[middle], hidden, precision=HIGHEST) + bias_mid[middle][:, None])
    shaped = jnp.dot(weight_out, hidden, precision=HIGHEST)
    scaled_pos = (positions.astype(jnp.float32) / length)[None, :]
    return shaped * jnp.exp(-decay_rate[:, None] * scaled_pos)

def normalized(raw):
    return raw / jnp.sqrt(lax.optimization_barrier(jnp.sum(raw * raw, axis=-1, keepdims=True)) + EPSILON)

def rounded(array):
    return lax.optimization_barrier(array.astype(jnp.bfloat16)).astype(jnp.float32)

def dft_tables(length):
    total = 2 * length
    col_count = 128
    row_count = total // col_count
    row_ids = jnp.arange(row_count, dtype=jnp.int32)
    half_ids = jnp.arange(row_count // 2, dtype=jnp.int32)
    col_ids = jnp.arange(col_count, dtype=jnp.int32)
    angle_rows = 2.0 * math.pi / row_count * (row_ids[:, None] * half_ids[None, :] % row_count).astype(jnp.float32)
    angle_cols = 2.0 * math.pi / col_count * (col_ids[:, None] * col_ids[None, :] % col_count).astype(jnp.float32)
    angle_twist = 2.0 * math.pi / total * (row_ids[:, None] * col_ids[None, :] % total).astype(jnp.float32)
    return (row_count, col_count, total, rounded(jnp.cos(angle_rows)), rounded(jnp.sin(angle_rows)), rounded(jnp.cos(angle_cols)), rounded(jnp.sin(angle_cols)), jnp.cos(angle_twist), jnp.sin(angle_twist))

def forward(signal, tables):
    row_count, col_count, total, cos_rows, sin_rows, cos_cols, sin_cols, cos_twist, sin_twist = tables
    shaped = rounded(signal.reshape(signal.shape[:-1] + (row_count // 2, col_count)))
    first_re = jnp.einsum('ka,...ab->...kb', cos_rows, shaped, precision=HIGHEST)
    first_im = -jnp.einsum('ka,...ab->...kb', sin_rows, shaped, precision=HIGHEST)
    twist_re = rounded(first_re * cos_twist + first_im * sin_twist)
    twist_im = rounded(first_im * cos_twist - first_re * sin_twist)
    spec_re = jnp.einsum('...kb,bq->...kq', twist_re, cos_cols, precision=HIGHEST) + jnp.einsum('...kb,bq->...kq', twist_im, sin_cols, precision=HIGHEST)
    spec_im = jnp.einsum('...kb,bq->...kq', twist_im, cos_cols, precision=HIGHEST) - jnp.einsum('...kb,bq->...kq', twist_re, sin_cols, precision=HIGHEST)
    return (spec_re, spec_im)

def inverse(spec_re, spec_im, tables):
    row_count, col_count, total, cos_rows, sin_rows, cos_cols, sin_cols, cos_twist, sin_twist = tables
    part_re = rounded(spec_re)
    part_im = rounded(spec_im)
    back_re = jnp.einsum('...kq,qb->...kb', part_re, cos_cols, precision=HIGHEST) - jnp.einsum('...kq,qb->...kb', part_im, sin_cols, precision=HIGHEST)
    back_im = jnp.einsum('...kq,qb->...kb', part_re, sin_cols, precision=HIGHEST) + jnp.einsum('...kq,qb->...kb', part_im, cos_cols, precision=HIGHEST)
    turn_re = rounded(back_re * cos_twist - back_im * sin_twist)
    turn_im = rounded(back_re * sin_twist + back_im * cos_twist)
    signal = jnp.einsum('ka,...kb->...ab', cos_rows, turn_re, precision=HIGHEST) - jnp.einsum('ka,...kb->...ab', sin_rows, turn_im, precision=HIGHEST)
    return signal.reshape(signal.shape[:-2] + (total // 2,)) / total

def reference(value, gate_in, gate_out, cotangent, skip_gain, weight_in, bias_in, weight_mid, bias_mid, weight_out, decay_rate):
    length = value.shape[-1]
    batch_count = value.shape[0]
    channels = value.shape[1]
    positions = jnp.arange(length, dtype=jnp.int32)

    def filter_all(wgt_in, bia_in, wgt_mid, bia_mid, wgt_out, rates):
        return normalized(filter_rows(wgt_in, bia_in, wgt_mid, bia_mid, wgt_out, rates, positions, length))
    kernel, pullback = jax.vjp(filter_all, weight_in, bias_in, weight_mid, bias_mid, weight_out, decay_rate)
    tables = dft_tables(length)
    kernel_re, kernel_im = forward(kernel, tables)

    def one_sequence(carry, inputs):
        kernel_sum, skip_sum = carry
        val_one, gin_one, gout_one, cot_one = inputs
        val_f = val_one.astype(jnp.float32)
        gin_f = gin_one.astype(jnp.float32)
        gout_f = gout_one.astype(jnp.float32)
        cot_f = cot_one.astype(jnp.float32)
        mixed = gin_f * val_f
        mixed_re, mixed_im = forward(mixed, tables)
        conv_re = mixed_re * kernel_re - mixed_im * kernel_im
        conv_im = mixed_re * kernel_im + mixed_im * kernel_re
        inner = inverse(conv_re, conv_im, tables) + skip_gain[:, None] * mixed
        grad_out = (cot_f * inner).astype(jnp.bfloat16)
        grad_inner = cot_f * gout_f
        inner_re, inner_im = forward(grad_inner, tables)
        back_re = inner_re * kernel_re + inner_im * kernel_im
        back_im = inner_im * kernel_re - inner_re * kernel_im
        grad_mixed = inverse(back_re, back_im, tables) + skip_gain[:, None] * grad_inner
        grad_val = (grad_mixed * gin_f).astype(jnp.bfloat16)
        grad_gin = (grad_mixed * val_f).astype(jnp.bfloat16)
        cross_re = mixed_re * inner_re + mixed_im * inner_im
        cross_im = mixed_re * inner_im - mixed_im * inner_re
        kernel_part = inverse(cross_re, cross_im, tables)
        carry_next = (kernel_sum + kernel_part, skip_sum + lax.optimization_barrier(jnp.sum(grad_inner * mixed, axis=-1)))
        return (carry_next, (grad_val, grad_gin, grad_out))
    start = (jnp.zeros((channels, length), jnp.float32), jnp.zeros((channels,), jnp.float32))
    final, stacked = lax.scan(one_sequence, start, (value, gate_in, gate_out, cotangent))
    grad_kernel, skip_sum = final
    grads = pullback(grad_kernel)
    factor = 1.0 / math.sqrt(batch_count * length)
    return (stacked[0], stacked[1], stacked[2], skip_sum * factor, grads[0] * factor, grads[1] * factor, grads[2] * factor, grads[3] * factor, grads[4] * factor, grads[5] * factor)
```

```python
import functools
import math

import jax
import jax.numpy as jnp
import numpy as np
from jax import lax
from jax.experimental import pallas as pl
from jax.experimental.pallas import tpu as pltpu
from jax.sharding import PartitionSpec as P

EPSILON = 1e-06
LANES = 128
F32 = jnp.float32
LOW = jnp.bfloat16


def band_table(length, bands):
    highest = length / 4.0
    return np.array(
        [math.floor(highest ** (number / (bands - 1)) + 0.5) for number in range(bands)], np.int32
    )


def feature_tables(length, bands, rows):
    freq = np.zeros((rows, LANES), np.int32)
    shift = np.zeros((rows, LANES), np.int32)
    table = band_table(length, bands)[:, None]
    freq[1 : 1 + bands] = table
    shift[1 : 1 + bands] = length // 4
    freq[1 + bands : 1 + 2 * bands] = table
    return freq, shift


def dft_tables(length):
    half = length // LANES
    rows = 2 * half
    k = np.arange(half)[:, None]
    a = np.arange(half)[None, :]
    angle = 2.0 * np.pi / rows * (k * a % rows)
    cos_rows = np.cos(angle)
    sin_rows = np.sin(angle)
    alternating = 1.0 - 2.0 * (np.arange(half) % 2)
    first = np.concatenate([cos_rows, -sin_rows], axis=0)
    first[half] = alternating
    weight = np.full((half, 1), 2.0)
    weight[0] = 1.0
    last = np.concatenate([cos_rows * weight, -sin_rows * weight], axis=0)
    last[half] = alternating
    last = last.T / (2.0 * length)
    col = np.arange(LANES)
    angle = 2.0 * np.pi / LANES * (col[:, None] * col[None, :] % LANES)
    cos_cols, sin_cols = np.cos(angle), np.sin(angle)
    ahead = np.block([[cos_cols, -sin_cols], [sin_cols, cos_cols]])
    back = np.block([[cos_cols, sin_cols], [-sin_cols, cos_cols]])
    total = 2 * length
    twist_rows = np.arange(half + 8)[:, None]
    angle = 2.0 * np.pi / total * (twist_rows * col[None, :] % total)
    low = lambda x: x.astype(np.float32).astype(LOW)
    return (
        low(first),
        low(ahead),
        low(back),
        low(last),
        np.cos(angle).astype(np.float32),
        np.sin(angle).astype(np.float32),
    )


def forward_pair(signal, tabs, r_ref, h_ref):
    first, ahead, cos_t, sin_t = tabs
    half = signal.shape[0]
    groups = half // 8
    r_ref[...] = jnp.dot(first[...], signal, preferred_element_type=F32)
    top = lax.broadcasted_iota(jnp.int32, (8, LANES), 0) == 0
    for g in range(groups + 1):
        cosine = cos_t[8 * g : 8 * g + 8, :]
        sine = sin_t[8 * g : 8 * g + 8, :]
        real, imag = [], []
        for c in range(2):
            lanes = slice(LANES * c, LANES * c + LANES)
            if g < groups:
                g_re = r_ref[8 * g : 8 * g + 8, lanes]
                g_im = r_ref[half + 8 * g : half + 8 * g + 8, lanes]
                if g == 0:
                    g_im = jnp.where(top, 0.0, g_im)
                real.append(g_re * cosine + g_im * sine)
                imag.append(g_im * cosine - g_re * sine)
            else:
                g_re = jnp.where(top, r_ref[half : half + 8, lanes], 0.0)
                real.append(g_re * cosine)
                imag.append(-(g_re * sine))
        rows = slice(16 * g, 16 * g + 16)
        h_ref[rows, :LANES] = jnp.concatenate(real, axis=0).astype(LOW)
        h_ref[rows, LANES:] = jnp.concatenate(imag, axis=0).astype(LOW)
    return jnp.dot(h_ref[...], ahead[...], preferred_element_type=F32)


def inverse_pair(s_ref, tabs, b_ref, t_ref):
    back, last, cos_t, sin_t = tabs
    half = last.shape[0]
    groups = half // 8
    b_ref[...] = jnp.dot(s_ref[...], back[...], preferred_element_type=F32)
    top = lax.broadcasted_iota(jnp.int32, (8, LANES), 0) == 0

    def turned(g, c):
        rows = slice(16 * g + 8 * c, 16 * g + 8 * c + 8)
        re, im = b_ref[rows, :LANES], b_ref[rows, LANES:]
        cosine = cos_t[8 * g : 8 * g + 8, :]
        sine = sin_t[8 * g : 8 * g + 8, :]
        return re * cosine - im * sine, re * sine + im * cosine

    for c in range(2):
        lanes = slice(LANES * c, LANES * c + LANES)
        for g in range(0, groups, 2):
            re0, im0 = turned(g, c)
            re1, im1 = turned(g + 1, c)
            if g == 0:
                im0 = jnp.where(top, turned(groups, c)[0], im0)
            t_ref[8 * g : 8 * g + 16, lanes] = jnp.concatenate([re0, re1], axis=0).astype(LOW)
            t_ref[half + 8 * g : half + 8 * g + 16, lanes] = jnp.concatenate(
                [im0, im1], axis=0
            ).astype(LOW)
    return jnp.dot(last[...], t_ref[...], preferred_element_type=F32)


def spectra_kernel(
    base_ref, val, gin, gout, cot, first, ahead, cos_t, sin_t,
    fm_out, fg_out, cross_out, skip_out,
    mix_s, grad_s, skip_s, r0, r1, h0, h1, *, chunks, seqs, chans,
):
    step = pl.program_id(0)
    chunk_rows = val.shape[2] // LANES
    half = chunk_rows * chunks

    @pl.when(step == 0)
    def _():
        skip_s[...] = jnp.zeros_like(skip_s)

    @pl.when(step < chunks)
    def _():
        for b in range(seqs):
            total = skip_s[...]
            for a in range(chunk_rows):
                lanes = slice(LANES * a, LANES * a + LANES)
                mixed = gin[b, :, lanes].astype(F32) * val[b, :, lanes].astype(F32)
                inner = cot[b, :, lanes].astype(F32) * gout[b, :, lanes].astype(F32)
                rows = pl.ds(pl.multiple_of((step * chunk_rows + a) * chans, chans), chans)
                mix_s[b, rows, :] = mixed
                grad_s[b, rows, :] = inner
                total = total + mixed * inner
            skip_s[...] = total

    @pl.when(step == chunks - 1)
    def _():
        per_row = jnp.sum(skip_s[...], axis=1, keepdims=True)
        lane = lax.broadcasted_iota(jnp.int32, (chans, LANES), 1)
        row = lax.broadcasted_iota(jnp.int32, (chans, LANES), 0)
        mine = lane == row + base_ref[0]
        spread = jnp.sum(jnp.where(mine, per_row, 0.0), axis=0, keepdims=True)
        top = lax.broadcasted_iota(jnp.int32, (8, LANES), 0) == 0
        skip_out[...] = jnp.where(top, spread, 0.0)

    @pl.when(step >= chunks)
    def _():
        pair = step - chunks
        tabs = (first, ahead, cos_t, sin_t)
        for b in range(seqs):
            def picked(ref):
                parts = [
                    ref[b, pl.ds(2 * pair + c, half, stride=chans), :] for c in range(2)
                ]
                return jnp.concatenate(parts, axis=1).astype(LOW)

            fm_out[b, 0] = forward_pair(picked(mix_s), tabs, r0, h0)
            fg_out[b, 0] = forward_pair(picked(grad_s), tabs, r1, h1)
        for g in range(half // 8 + 1):
            rows = slice(16 * g, 16 * g + 16)
            cross_re = cross_im = None
            for b in range(seqs):
                m_re, m_im = fm_out[b, 0, rows, :LANES], fm_out[b, 0, rows, LANES:]
                g_re, g_im = fg_out[b, 0, rows, :LANES], fg_out[b, 0, rows, LANES:]
                c_re = m_re * g_re + m_im * g_im
                c_im = m_re * g_im - m_im * g_re
                cross_re = c_re if b == 0 else cross_re + c_re
                cross_im = c_im if b == 0 else cross_im + c_im
            cross_out[0, rows, :LANES] = cross_re.astype(LOW)
            cross_out[0, rows, LANES:] = cross_im.astype(LOW)


def kernel_kernel(
    base_ref, cross, raw, first, ahead, back, last, cos_t, sin_t,
    fk_out, grad_out, rate_out,
    r0, h0, b0, t0, *, length,
):
    pair = pl.program_id(0)
    blocks, _, rows_each, _ = raw.shape
    half = blocks * rows_each
    lane = lax.broadcasted_iota(jnp.int32, (8, LANES), 1)
    top = lax.broadcasted_iota(jnp.int32, (8, LANES), 0) == 0
    position = (
        lax.broadcasted_iota(jnp.int32, (half, LANES), 0) * LANES
        + lax.broadcasted_iota(jnp.int32, (half, LANES), 1)
    ).astype(F32) * (-1.0 / length)

    @pl.when(pair == 0)
    def _():
        rate_out[...] = jnp.zeros_like(rate_out)

    shaped, norms = [], []
    for c in range(2):
        row = raw[:, c].reshape(half, LANES)
        norm = jnp.sqrt(jnp.sum(row * row, keepdims=True) + EPSILON)
        norms.append(norm)
        shaped.append(row / norm)
    signal = jnp.concatenate(shaped, axis=1).astype(LOW)
    fk_out[0] = forward_pair(signal, (first, ahead, cos_t, sin_t), r0, h0)
    grads = inverse_pair(cross.at[0], (back, last, cos_t, sin_t), b0, t0)
    for c in range(2):
        row = raw[:, c].reshape(half, LANES)
        grad = grads[:, LANES * c : LANES * c + LANES]
        norm = norms[c]
        along = jnp.sum(row * grad, keepdims=True)
        grad_raw = grad / norm - row * (along / (norm * norm * norm))
        grad_out[:, c] = grad_raw.reshape(blocks, rows_each, LANES)
        rate = jnp.sum(grad_raw * row * position, keepdims=True)
        mine = jnp.logical_and(lane == base_ref[0] + 2 * pair + c, top)
        rate_out[...] = rate_out[...] + jnp.where(mine, rate, 0.0)


def output_kernel(
    fm, fg, fk, val, gin, gout, cot, skip, back, last, cos_t, sin_t,
    val_out, gin_out, gout_out,
    conv_s, corr_s, s0, s1, b0, b1, t0, t1, *, pairs, chunks, seqs, chans,
):
    step = pl.program_id(0)
    chunk_rows = val.shape[2] // LANES
    half = chunk_rows * chunks

    @pl.when(step < pairs)
    def _():
        tabs = (back, last, cos_t, sin_t)
        for b in range(seqs):
            for g in range(half // 8 + 1):
                rows = slice(16 * g, 16 * g + 16)
                k_re, k_im = fk[0, rows, :LANES], fk[0, rows, LANES:]
                m_re, m_im = fm[b, 0, rows, :LANES], fm[b, 0, rows, LANES:]
                s0[rows, :LANES] = (m_re * k_re - m_im * k_im).astype(LOW)
                s0[rows, LANES:] = (m_re * k_im + m_im * k_re).astype(LOW)
                g_re, g_im = fg[b, 0, rows, :LANES], fg[b, 0, rows, LANES:]
                s1[rows, :LANES] = (g_re * k_re + g_im * k_im).astype(LOW)
                s1[rows, LANES:] = (g_im * k_re - g_re * k_im).astype(LOW)
            conv = inverse_pair(s0, tabs, b0, t0)
            corr = inverse_pair(s1, tabs, b1, t1)
            for c in range(2):
                lanes = slice(LANES * c, LANES * c + LANES)
                conv_s[b, pl.ds(2 * step + c, half, stride=chans), :] = conv[:, lanes]
                corr_s[b, pl.ds(2 * step + c, half, stride=chans), :] = corr[:, lanes]

    @pl.when(step >= pairs)
    def _():
        chunk = step - pairs
        lane = lax.broadcasted_iota(jnp.int32, (chans, LANES), 1)
        row = lax.broadcasted_iota(jnp.int32, (chans, LANES), 0)
        gain = jnp.sum(jnp.where(lane == row, skip[0:1, :], 0.0), axis=1, keepdims=True)
        gain = jnp.broadcast_to(gain, (chans, LANES))
        for b in range(seqs):
            for a in range(chunk_rows):
                lanes = slice(LANES * a, LANES * a + LANES)
                rows = pl.ds(pl.multiple_of((chunk * chunk_rows + a) * chans, chans), chans)
                v = val[b, :, lanes].astype(F32)
                gi = gin[b, :, lanes].astype(F32)
                go = gout[b, :, lanes].astype(F32)
                co = cot[b, :, lanes].astype(F32)
                inner = conv_s[b, rows, :] + gain * (gi * v)
                grad_mixed = corr_s[b, rows, :] + gain * (co * go)
                gout_out[b, :, lanes] = (co * inner).astype(LOW)
                val_out[b, :, lanes] = (grad_mixed * gi).astype(LOW)
                gin_out[b, :, lanes] = (grad_mixed * v).astype(LOW)


INV_PI = 0.3183098861837907
PI_HIGH = 3.140625
PI_MID = 9.67502593994140625e-4
PI_LOW = 1.509957990978376432e-7


def sine_poly(r, r2):
    p = 2.7557319e-06 + r2 * -2.50507e-08
    p = -1.98412698e-04 + r2 * p
    p = 8.33333333e-03 + r2 * p
    p = -1.66666667e-01 + r2 * p
    return r + r * (r2 * p)


def cosine_poly(r2):
    p = -2.7557319e-07 + r2 * 2.0876757e-09
    p = 2.48015873e-05 + r2 * p
    p = -1.38888889e-03 + r2 * p
    p = 4.16666667e-02 + r2 * p
    p = -0.5 + r2 * p
    return 1.0 + r2 * p


def sine_cosine(z):
    turns = jnp.floor(z * INV_PI + 0.5)
    r = ((z - turns * PI_HIGH) - turns * PI_MID) - turns * PI_LOW
    sign = 1.0 - 2.0 * (turns - 2.0 * jnp.floor(turns * 0.5))
    r2 = r * r
    return sign * sine_poly(r, r2), sign * cosine_poly(r2)


def column(row, size):
    lane = lax.broadcasted_iota(jnp.int32, (size, size), 1)
    diagonal = lane == lax.broadcasted_iota(jnp.int32, (size, size), 0)
    return jnp.sum(jnp.where(diagonal, row, 0.0), axis=1, keepdims=True)


def split(x):
    high = x.astype(LOW)
    return high, (x - high.astype(F32)).astype(LOW)


def triple_dot(weight, x):
    w_high, w_low = split(weight)
    x_high, x_low = split(x)
    dot = functools.partial(jnp.dot, preferred_element_type=F32)
    return dot(w_high, x_high) + (dot(w_high, x_low) + dot(w_low, x_high))


def filter_kernel(
    start_ref, freq, shift, w_in, b_in, w_mid, b_mid, w_out, rates,
    raw_out, feat_out, act_out, cos_out, *, length,
):
    width = feat_out.shape[1]
    order = w_in.shape[0]
    start = start_ref[0] + pl.program_id(0) * width
    rows = freq.shape[0]
    position = start + lax.broadcasted_iota(jnp.int32, (rows, width), 1)
    freq_w = jnp.concatenate([freq[...]] * (width // LANES), axis=1)
    shift_w = jnp.concatenate([shift[...]] * (width // LANES), axis=1)
    quarter = length // 4
    phase = position * freq_w + shift_w + quarter
    sign = (1 - ((phase >> int(math.log2(length // 2))) & 1) * 2).astype(F32)
    angle = ((phase & (length // 2 - 1)) - quarter).astype(F32) * (2.0 * math.pi / length)
    wave = sign * sine_poly(angle, angle * angle)
    linear = lax.broadcasted_iota(jnp.int32, (rows, width), 0) == 0
    feature = jnp.where(linear, position.astype(F32) * (1.0 / length), wave)
    feat_out[...] = feature.astype(LOW)

    def layer(weight, x, bias, number):
        z = triple_dot(weight, x) + column(bias, order)
        sine, cosine = sine_cosine(z)
        act_out[order * number : order * number + order, :] = sine.astype(LOW)
        cos_out[order * number : order * number + order, :] = cosine
        return sine

    hidden = layer(w_in[...], feature, b_in[...], 0)
    hidden = layer(w_mid[0], hidden, b_mid[0:1, :], 1)
    hidden = layer(w_mid[1], hidden, b_mid[1:2, :], 2)
    shaped = triple_dot(w_out[...], hidden)
    channels = w_out.shape[0]
    rate = column(rates[...], channels) * (-1.0 / length)
    lane = lax.broadcasted_iota(jnp.int32, (channels, LANES), 1)
    for a in range(width // LANES):
        where = (start + a * LANES + lane).astype(F32)
        raw_out[:, a, :] = shaped[:, LANES * a : LANES * a + LANES] * jnp.exp(rate * where)


def nt_dot(x, y):
    return lax.dot_general(x, y, (((1,), (1,)), ((), ())), preferred_element_type=F32)


def tn_triple(weight, x):
    w_high, w_low = split(weight.T)
    x_high, x_low = split(x)
    dot = functools.partial(jnp.dot, preferred_element_type=F32)
    return dot(w_high, x_high) + (dot(w_high, x_low) + dot(w_low, x_high))


def filter_grad_kernel(
    start_ref, grad, feat, act, cosines, w_mid, w_out, rates, rate_row, skip_row,
    packed, d_out, d_mid, d_in, d_bias, *, length,
):
    step = pl.program_id(0)
    width = feat.shape[1]
    order = w_mid.shape[1]
    channels = w_out.shape[0]
    start = start_ref[0] + step * width

    @pl.when(step == 0)
    def _():
        for ref in (d_out, d_mid, d_in, d_bias):
            ref[...] = jnp.zeros_like(ref)

    rate = column(rates[...], channels) * (-1.0 / length)
    lane = lax.broadcasted_iota(jnp.int32, (channels, LANES), 1)
    parts = []
    for a in range(width // LANES):
        where = (start + a * LANES + lane).astype(F32)
        parts.append(grad[:, a, :] * jnp.exp(rate * where))
    d_shaped = jnp.concatenate(parts, axis=1)

    def part(ref, number):
        return ref[order * number : order * number + order, :]

    def bias_sum(x, number):
        total = x[:, :LANES]
        for a in range(1, width // LANES):
            total = total + x[:, LANES * a : LANES * a + LANES]
        d_bias[number] = d_bias[number] + total

    d_out[...] = d_out[...] + nt_dot(d_shaped.astype(LOW), part(act, 2))
    dz = tn_triple(w_out[...], d_shaped) * part(cosines, 2)
    bias_sum(dz, 2)
    d_mid[1] = d_mid[1] + nt_dot(dz.astype(LOW), part(act, 1))
    dz = tn_triple(w_mid[1], dz) * part(cosines, 1)
    bias_sum(dz, 1)
    d_mid[0] = d_mid[0] + nt_dot(dz.astype(LOW), part(act, 0))
    dz = tn_triple(w_mid[0], dz) * part(cosines, 0)
    bias_sum(dz, 0)
    d_in[...] = d_in[...] + nt_dot(dz.astype(LOW), feat[...])

    @pl.when(step == pl.num_programs(0) - 1)
    def _():
        packed[...] = jnp.zeros_like(packed)
        packed[:channels, :order] = d_out[...]
        base = channels
        packed[base : base + order, :order] = d_mid[0]
        packed[base + order : base + 2 * order, :order] = d_mid[1]
        base += 2 * order
        features = d_in.shape[1]
        packed[base : base + order, :features] = d_in[...]
        spot = lax.broadcasted_iota(jnp.int32, (order, LANES), 1)
        current = packed[base : base + order, :]
        for number in range(3):
            total = jnp.sum(d_bias[number], axis=1, keepdims=True)
            current = jnp.where(spot == features + number, total, current)
        packed[base : base + order, :] = current
        base += order
        packed[base : base + 8, :] = rate_row[...]
        packed[base + 8 : base + 16, :] = skip_row[...]


def unpack_kernel(pieces, w_in, b_in, w_mid, b_mid, w_out, rate, skip, *, scale, features):
    total = pieces[0]
    for number in range(1, pieces.shape[0]):
        total = total + pieces[number]
    total = total * scale
    channels, order = w_out.shape
    w_out[...] = total[:channels, :order]
    base = channels
    w_mid[0] = total[base : base + order, :order]
    w_mid[1] = total[base + order : base + 2 * order, :order]
    base += 2 * order
    block = total[base : base + order, :]
    w_in[...] = block[:, : w_in.shape[1]]
    lane = lax.broadcasted_iota(jnp.int32, (order, LANES), 1)
    row = lax.broadcasted_iota(jnp.int32, (order, LANES), 0)

    def as_row(number):
        values = jnp.sum(jnp.where(lane == features + number, block, 0.0), axis=1, keepdims=True)
        return jnp.sum(jnp.where(lane == row, values, 0.0), axis=0, keepdims=True)[:, :order]

    b_in[...] = as_row(0)
    b_mid[0:1, :] = as_row(1)
    b_mid[1:2, :] = as_row(2)
    base += order
    rate[...] = total[base : base + 1, :]
    skip[...] = total[base + 8 : base + 9, :]


def const_spec(array):
    zeros = (0,) * len(array.shape)
    return pl.BlockSpec(array.shape, lambda i: zeros)


SCALAR = pl.BlockSpec(memory_space=pltpu.SMEM)


def vmem(shape, dtype=F32):
    return pltpu.VMEM(shape, dtype)


def shape(dims, dtype=F32):
    return jax.ShapeDtypeStruct(dims, dtype)


def fan_in(x, axis):
    size = lax.axis_size(axis)
    parts = [x]
    for d in range(1, size):
        parts.append(lax.ppermute(x, axis, [(s, (s + d) % size) for s in range(size)]))
    return parts


def local(
    value, gate_in, gate_out, cotangent, skip_gain,
    weight_in, bias_in, weight_mid, bias_mid, weight_out, decay_rate,
):
    seqs, chans, length = value.shape
    channels, order = weight_out.shape
    chan_count = lax.axis_size("chan")
    seq_count = lax.axis_size("seq")
    block = length // chan_count
    block_rows = block // LANES
    half = length // LANES
    pairs = chans // 2
    spec_rows = 2 * (half + 8)
    chunks = 8
    start = (lax.axis_index("chan") * block).astype(jnp.int32).reshape(1)
    base = (lax.axis_index("chan") * chans).astype(jnp.int32).reshape(1)
    first, ahead, back, last, cos_t, sin_t = [jnp.asarray(t) for t in dft_tables(length)]
    feature_rows = 48
    bands = (weight_in.shape[1] - 1) // 2
    freq, shift = [jnp.asarray(t) for t in feature_tables(length, bands, feature_rows)]

    width = min(1024, block)
    steps = block // width
    rates = decay_rate.reshape(1, channels)
    w_in_wide = jnp.pad(weight_in, ((0, 0), (0, feature_rows - weight_in.shape[1])))
    weights = (w_in_wide, bias_in.reshape(1, order), weight_mid, bias_mid, weight_out, rates)
    raw_block, feats, acts, cosines = pl.pallas_call(
        functools.partial(filter_kernel, length=length),
        grid=(steps,),
        in_specs=[SCALAR] + [const_spec(x) for x in (freq, shift) + weights],
        out_specs=[
            pl.BlockSpec((channels, width // LANES, LANES), lambda i: (0, i, 0)),
            pl.BlockSpec((feature_rows, width), lambda i: (0, i)),
            pl.BlockSpec((3 * order, width), lambda i: (0, i)),
            pl.BlockSpec((3 * order, width), lambda i: (0, i)),
        ],
        out_shape=[
            shape((channels, block_rows, LANES)),
            shape((feature_rows, block), LOW),
            shape((3 * order, block), LOW),
            shape((3 * order, block)),
        ],
        name="filter_rows",
    )(start, freq, shift, *weights)
    raw = lax.all_to_all(
        raw_block.reshape(chan_count, chans, block_rows, LANES),
        "chan", split_axis=0, concat_axis=0, tiled=True,
    )

    chunk = length // chunks
    ahead_tabs = (first, ahead, cos_t, sin_t)
    early = lambda i: (0, 0, jnp.minimum(i, chunks - 1))
    late = lambda i: (0, jnp.maximum(i - chunks, 0), 0, 0)
    fm, fg, cross, skip_row = pl.pallas_call(
        functools.partial(spectra_kernel, chunks=chunks, seqs=seqs, chans=chans),
        grid=(chunks + pairs,),
        in_specs=[SCALAR]
        + [pl.BlockSpec((seqs, chans, chunk), early)] * 4
        + [const_spec(x) for x in ahead_tabs],
        out_specs=[
            pl.BlockSpec((seqs, 1, spec_rows, 2 * LANES), late),
            pl.BlockSpec((seqs, 1, spec_rows, 2 * LANES), late),
            pl.BlockSpec((1, spec_rows, 2 * LANES), lambda i: (jnp.maximum(i - chunks, 0), 0, 0)),
            pl.BlockSpec((8, LANES), lambda i: (0, 0)),
        ],
        out_shape=[
            shape((seqs, pairs, spec_rows, 2 * LANES)),
            shape((seqs, pairs, spec_rows, 2 * LANES)),
            shape((pairs, spec_rows, 2 * LANES), LOW),
            shape((8, LANES)),
        ],
        scratch_shapes=[
            vmem((seqs, half * chans, LANES)),
            vmem((seqs, half * chans, LANES)),
            vmem((chans, LANES)),
            vmem((2 * half, 2 * LANES)),
            vmem((2 * half, 2 * LANES)),
            vmem((spec_rows, 2 * LANES), LOW),
            vmem((spec_rows, 2 * LANES), LOW),
        ],
        name="spectra",
    )(base, value, gate_in, gate_out, cotangent, *ahead_tabs)

    tables = (first, ahead, back, last, cos_t, sin_t)
    fk, grad_raw, rate_row = pl.pallas_call(
        functools.partial(kernel_kernel, length=length),
        grid=(pairs,),
        in_specs=[
            SCALAR,
            pl.BlockSpec((1, spec_rows, 2 * LANES), lambda i: (i, 0, 0)),
            pl.BlockSpec((chan_count, 2, block_rows, LANES), lambda i: (0, i, 0, 0)),
        ]
        + [const_spec(x) for x in tables],
        out_specs=[
            pl.BlockSpec((1, spec_rows, 2 * LANES), lambda i: (i, 0, 0)),
            pl.BlockSpec((chan_count, 2, block_rows, LANES), lambda i: (0, i, 0, 0)),
            pl.BlockSpec((8, LANES), lambda i: (0, 0)),
        ],
        out_shape=[
            shape((pairs, spec_rows, 2 * LANES)),
            shape((chan_count, chans, block_rows, LANES)),
            shape((8, LANES)),
        ],
        scratch_shapes=[
            vmem((2 * half, 2 * LANES)),
            vmem((spec_rows, 2 * LANES), LOW),
            vmem((spec_rows, 2 * LANES)),
            vmem((2 * half, 2 * LANES), LOW),
        ],
        name="filter_spectrum",
    )(base, cross, raw, *tables)
    grad_block = lax.all_to_all(grad_raw, "chan", split_axis=0, concat_axis=0, tiled=True)

    skip_wide = jnp.pad(skip_gain.reshape(1, chans), ((0, 7), (0, LANES - chans)))
    back_tabs = (back, last, cos_t, sin_t)
    early4 = lambda i: (0, jnp.minimum(i, pairs - 1), 0, 0)
    late3 = lambda i: (0, 0, jnp.maximum(i - pairs, 0))
    signal_spec = pl.BlockSpec((seqs, chans, chunk), late3)
    grad_val, grad_gin, grad_gout = pl.pallas_call(
        functools.partial(output_kernel, pairs=pairs, chunks=chunks, seqs=seqs, chans=chans),
        grid=(pairs + chunks,),
        in_specs=[
            pl.BlockSpec((seqs, 1, spec_rows, 2 * LANES), early4),
            pl.BlockSpec((seqs, 1, spec_rows, 2 * LANES), early4),
            pl.BlockSpec((1, spec_rows, 2 * LANES), lambda i: (jnp.minimum(i, pairs - 1), 0, 0)),
        ]
        + [signal_spec] * 4
        + [const_spec(x) for x in (skip_wide,) + back_tabs],
        out_specs=[signal_spec] * 3,
        out_shape=[shape((seqs, chans, length), LOW)] * 3,
        scratch_shapes=[
            vmem((seqs, half * chans, LANES)),
            vmem((seqs, half * chans, LANES)),
            vmem((spec_rows, 2 * LANES), LOW),
            vmem((spec_rows, 2 * LANES), LOW),
            vmem((spec_rows, 2 * LANES)),
            vmem((spec_rows, 2 * LANES)),
            vmem((2 * half, 2 * LANES), LOW),
            vmem((2 * half, 2 * LANES), LOW),
        ],
        name="outputs",
    )(fm, fg, fk, value, gate_in, gate_out, cotangent, skip_wide, *back_tabs)

    packed_rows = channels + 3 * order + 16
    grad_in = grad_block.reshape(channels, block_rows, LANES)
    packed = pl.pallas_call(
        functools.partial(filter_grad_kernel, length=length),
        grid=(steps,),
        in_specs=[
            SCALAR,
            pl.BlockSpec((channels, width // LANES, LANES), lambda i: (0, i, 0)),
            pl.BlockSpec((feature_rows, width), lambda i: (0, i)),
            pl.BlockSpec((3 * order, width), lambda i: (0, i)),
            pl.BlockSpec((3 * order, width), lambda i: (0, i)),
        ]
        + [const_spec(x) for x in (weight_mid, weight_out, rates, rate_row, skip_row)],
        out_specs=pl.BlockSpec((packed_rows, LANES), lambda i: (0, 0)),
        out_shape=shape((packed_rows, LANES)),
        scratch_shapes=[
            vmem((channels, order)),
            vmem((2, order, order)),
            vmem((order, feature_rows)),
            vmem((3, order, LANES)),
        ],
        name="filter_gradients",
    )(start, grad_in, feats, acts, cosines, weight_mid, weight_out, rates, rate_row, skip_row)

    group = functools.reduce(jnp.add, fan_in(packed, "chan"))
    pieces = jnp.stack(fan_in(group, "seq"))
    factor = 1.0 / math.sqrt(seqs * seq_count * length)
    d_in, d_bin, d_mid, d_bmid, d_out, d_rate, d_skip = pl.pallas_call(
        functools.partial(unpack_kernel, scale=factor, features=feature_rows),
        out_shape=[
            shape(weight_in.shape),
            shape((1, order)),
            shape(weight_mid.shape),
            shape(bias_mid.shape),
            shape(weight_out.shape),
            shape((1, LANES)),
            shape((1, LANES)),
        ],
        name="unpack",
    )(pieces)
    skip_total = lax.dynamic_slice(d_skip[0], (base[0],), (chans,))
    return (
        grad_val, grad_gin, grad_gout, skip_total,
        d_in, d_bin[0], d_mid, d_bmid, d_out, d_rate[0, :channels],
    )


def solution(mesh):
    large = P("seq", "chan", None)
    return jax.shard_map(
        local,
        mesh=mesh,
        in_specs=(large,) * 4 + (P("chan"),) + (P(),) * 6,
        out_specs=(large,) * 3 + (P("chan"),) + (P(),) * 6,
        check_vma=False,
    )
```

```python
import functools
import math

import jax
import jax.numpy as jnp
import numpy as np
from jax import lax
from jax.experimental import pallas as pl
from jax.experimental.pallas import tpu as pltpu
from jax.sharding import PartitionSpec as P

EPSILON = 1e-06
LANES = 128
F32 = jnp.float32
LOW = jnp.bfloat16


def band_table(length, bands):
    highest = length / 4.0
    return np.array(
        [math.floor(highest ** (number / (bands - 1)) + 0.5) for number in range(bands)], np.int32
    )


def feature_tables(length, bands, rows):
    freq = np.zeros((rows, LANES), np.int32)
    shift = np.full((rows, LANES), length // 4, np.int32)
    table = band_table(length, bands)[:, None]
    freq[1 : 1 + bands] = table
    shift[1 : 1 + bands] = length // 2
    freq[1 + bands : 1 + 2 * bands] = table
    return freq, shift


def dft_tables(length):
    half = length // LANES
    rows = 2 * half
    k = np.arange(half)[:, None]
    a = np.arange(half)[None, :]
    angle = 2.0 * np.pi / rows * (k * a % rows)
    cos_rows = np.cos(angle)
    sin_rows = np.sin(angle)
    alternating = 1.0 - 2.0 * (np.arange(half) % 2)
    first = np.concatenate([cos_rows, -sin_rows], axis=0)
    first[half] = alternating
    weight = np.full((half, 1), 2.0)
    weight[0] = 1.0
    last = np.concatenate([cos_rows * weight, -sin_rows * weight], axis=0)
    last[half] = alternating
    last = last.T / (2.0 * length)
    col = np.arange(LANES)
    angle = 2.0 * np.pi / LANES * (col[:, None] * col[None, :] % LANES)
    cos_cols, sin_cols = np.cos(angle), np.sin(angle)
    ahead = np.block([[cos_cols, -sin_cols], [sin_cols, cos_cols]])
    back = np.block([[cos_cols, sin_cols], [-sin_cols, cos_cols]])
    total = 2 * length
    twist_rows = np.arange(half + 8)[:, None]
    angle = 2.0 * np.pi / total * (twist_rows * col[None, :] % total)
    low = lambda x: x.astype(np.float32).astype(LOW)
    return (
        low(first),
        low(ahead),
        low(back),
        low(last),
        np.cos(angle).astype(np.float32),
        np.sin(angle).astype(np.float32),
    )


def forward_rows(signal, tabs, r_ref):
    r_ref[...] = jnp.dot(tabs[0][...], signal, preferred_element_type=F32)


def forward_columns(tabs, h_ref):
    return jnp.dot(h_ref[...], tabs[1][...], preferred_element_type=F32)


def forward_pair(signal, tabs, r_ref, h_ref):
    forward_rows(signal, tabs, r_ref)
    forward_twist(tabs, r_ref, h_ref)
    return forward_columns(tabs, h_ref)


def forward_twist(tabs, r_ref, h_ref):
    first, ahead, cos_t, sin_t = tabs
    half = first.shape[1]
    groups = half // 8
    top = lax.broadcasted_iota(jnp.int32, (8, LANES), 0) == 0
    for g in range(groups + 1):
        cosine = cos_t[8 * g : 8 * g + 8, :]
        sine = sin_t[8 * g : 8 * g + 8, :]
        real, imag = [], []
        for c in range(2):
            lanes = slice(LANES * c, LANES * c + LANES)
            if g < groups:
                g_re = r_ref[8 * g : 8 * g + 8, lanes]
                g_im = r_ref[half + 8 * g : half + 8 * g + 8, lanes]
                if g == 0:
                    g_im = jnp.where(top, 0.0, g_im)
                real.append(g_re * cosine + g_im * sine)
                imag.append(g_im * cosine - g_re * sine)
            else:
                g_re = jnp.where(top, r_ref[half : half + 8, lanes], 0.0)
                real.append(g_re * cosine)
                imag.append(-(g_re * sine))
        rows = slice(16 * g, 16 * g + 16)
        h_ref[rows, :LANES] = jnp.concatenate(real, axis=0).astype(LOW)
        h_ref[rows, LANES:] = jnp.concatenate(imag, axis=0).astype(LOW)


def inverse_columns(s_ref, tabs, b_ref):
    b_ref[...] = jnp.dot(s_ref[...], tabs[0][...], preferred_element_type=F32)


def inverse_twist(tabs, b_ref, t_ref):
    _, last, cos_t, sin_t = tabs
    half = last.shape[0]
    groups = half // 8
    top = lax.broadcasted_iota(jnp.int32, (8, LANES), 0) == 0

    def turned(g, c):
        rows = slice(16 * g + 8 * c, 16 * g + 8 * c + 8)
        re, im = b_ref[rows, :LANES], b_ref[rows, LANES:]
        cosine = cos_t[8 * g : 8 * g + 8, :]
        sine = sin_t[8 * g : 8 * g + 8, :]
        return re * cosine - im * sine, re * sine + im * cosine

    for g in range(0, groups, 2):
        for c in range(2):
            lanes = slice(LANES * c, LANES * c + LANES)
            re0, im0 = turned(g, c)
            re1, im1 = turned(g + 1, c)
            if g == 0:
                im0 = jnp.where(top, turned(groups, c)[0], im0)
            t_ref[8 * g : 8 * g + 16, lanes] = jnp.concatenate([re0, re1], axis=0).astype(LOW)
            t_ref[half + 8 * g : half + 8 * g + 16, lanes] = jnp.concatenate(
                [im0, im1], axis=0
            ).astype(LOW)


def inverse_rows(tabs, t_ref):
    return jnp.dot(tabs[1][...], t_ref[...], preferred_element_type=F32)


def inverse_pair(s_ref, tabs, b_ref, t_ref):
    inverse_columns(s_ref, tabs, b_ref)
    inverse_twist(tabs, b_ref, t_ref)
    return inverse_rows(tabs, t_ref)


def staggered(jobs):
    stages = max(len(job) for job in jobs)
    for when in range(len(jobs) + stages - 1):
        for number in reversed(range(len(jobs))):
            stage = when - number
            if 0 <= stage < len(jobs[number]):
                jobs[number][stage]()


def spectra_kernel(
    base_ref, val, gin, gout, cot, first, ahead, back, last, cos_t, sin_t,
    fm_out, fg_out, skip_out, grad_out,
    mix_s, grad_s, skip_s, r_s, h_s, f_s, cross_s, b_s, t_s, *, chunks, seqs, chans,
):
    step = pl.program_id(0)
    chunk_rows = val.shape[2] // LANES
    half = chunk_rows * chunks

    @pl.when(step == 0)
    def _():
        skip_s[...] = jnp.zeros_like(skip_s)

    @pl.when(step < chunks)
    def _():
        for b in range(seqs):
            total = skip_s[...]
            for a in range(chunk_rows):
                lanes = slice(LANES * a, LANES * a + LANES)
                mixed = gin[b, :, lanes].astype(F32) * val[b, :, lanes].astype(F32)
                inner = cot[b, :, lanes].astype(F32) * gout[b, :, lanes].astype(F32)
                rows = pl.ds((step * chunk_rows + a) * (chans + 1), chans)
                mix_s[b, rows, :] = mixed
                grad_s[b, rows, :] = inner
                total = total + mixed * inner
            skip_s[...] = total

    @pl.when(step == chunks - 1)
    def _():
        per_row = jnp.sum(skip_s[...], axis=1, keepdims=True)
        lane = lax.broadcasted_iota(jnp.int32, (chans, LANES), 1)
        row = lax.broadcasted_iota(jnp.int32, (chans, LANES), 0)
        mine = lane == row + base_ref[0]
        spread = jnp.sum(jnp.where(mine, per_row, 0.0), axis=0, keepdims=True)
        top = lax.broadcasted_iota(jnp.int32, (8, LANES), 0) == 0
        skip_out[...] = jnp.where(top, spread, 0.0)

    @pl.when(step >= chunks)
    def _():
        pair = step - chunks
        tabs = (first, ahead, cos_t, sin_t)

        def job(number):
            b, inner = number // 2, number % 2 == 1
            source, target = (grad_s, fg_out) if inner else (mix_s, fm_out)
            r_ref, h_ref = r_s.at[number], h_s.at[number]

            def rows():
                parts = [
                    source[b, pl.ds(2 * pair + c, half, stride=chans + 1), :] for c in range(2)
                ]
                forward_rows(jnp.concatenate(parts, axis=1).astype(LOW), tabs, r_ref)

            def twist():
                forward_twist(tabs, r_ref, h_ref)

            def columns():
                f_s[number] = forward_columns(tabs, h_ref)
                target[b, 0] = f_s[number].astype(LOW)

            return rows, twist, columns

        staggered([job(number) for number in range(2 * seqs)])
        for g in range(half // 8 + 1):
            rows = slice(16 * g, 16 * g + 16)
            cross_re = cross_im = None
            for b in range(seqs):
                m_re, m_im = f_s[2 * b, rows, :LANES], f_s[2 * b, rows, LANES:]
                g_re, g_im = f_s[2 * b + 1, rows, :LANES], f_s[2 * b + 1, rows, LANES:]
                c_re = m_re * g_re + m_im * g_im
                c_im = m_re * g_im - m_im * g_re
                cross_re = c_re if b == 0 else cross_re + c_re
                cross_im = c_im if b == 0 else cross_im + c_im
            cross_s[rows, :LANES] = cross_re.astype(LOW)
            cross_s[rows, LANES:] = cross_im.astype(LOW)
        y = inverse_pair(cross_s, (back, last, cos_t, sin_t), b_s, t_s)
        members, _, each, _ = grad_out.shape
        for c in range(2):
            lanes = slice(LANES * c, LANES * c + LANES)
            grad_out[:, c] = y[:, lanes].reshape(members, each, LANES)


def kernel_kernel(
    base_ref, raw, grads, first, ahead, cos_t, sin_t, fk_out, grad_out, lines_out, r_s, h_s, *, length,
):
    step = pl.program_id(0)
    blocks, channels, rows_each, _ = raw.shape
    half = blocks * rows_each
    lane = lax.broadcasted_iota(jnp.int32, (8, LANES), 1)
    line = lax.broadcasted_iota(jnp.int32, (8, LANES), 0)
    position = (
        lax.broadcasted_iota(jnp.int32, (half, LANES), 0) * LANES
        + lax.broadcasted_iota(jnp.int32, (half, LANES), 1)
    ).astype(F32) * (-1.0 / length)
    tabs = (first, ahead, cos_t, sin_t)

    @pl.when(step == 0)
    def _():
        lines_out[...] = jnp.zeros_like(lines_out)

    def job(number):
        def rows():
            parts = [raw[:, 2 * number + c].reshape(half, LANES) for c in range(2)]
            signal = jnp.concatenate(parts, axis=1).astype(LOW)
            forward_rows(signal, tabs, r_s.at[number])

        def twist():
            forward_twist(tabs, r_s.at[number], h_s.at[number])

        def columns():
            fk_out[number] = forward_columns(tabs, h_s.at[number]).astype(LOW)

        return rows, twist, columns

    staggered([job(number) for number in range(channels // 2)])
    total = lines_out[...]
    for c in range(channels):
        row, grad = raw[:, c].reshape(half, LANES), grads[:, c].reshape(half, LANES)
        square = jnp.sum(row * row, keepdims=True) + EPSILON
        inv = 1.0 / jnp.sqrt(square)
        coef = jnp.sum(row * grad, keepdims=True) * (inv / square)
        grad_raw = grad * inv - row * coef
        grad_out[:, c] = grad_raw.reshape(blocks, rows_each, LANES)
        rate = jnp.sum(grad_raw * row * position, keepdims=True)
        mine = lane == base_ref[0] + channels * step + c
        for number, x in enumerate((inv, rate)):
            total = jnp.where(jnp.logical_and(mine, line == number), x, total)
    lines_out[...] = total


def output_kernel(
    base_ref, fm, fg, fk, val, gin, gout, cot, skip, lines, back, last, cos_t, sin_t, *rest,
    steps, chunks, chans,
):
    val_out, gin_out, gout_out, token, conv_s, corr_s, s_s, b_s, t_s = rest[-9:]
    step = pl.program_id(0)
    chunk_rows = val.shape[2] // LANES
    half = chunk_rows * chunks
    together = fk.shape[0]

    @pl.when(step < steps)
    def _():
        tabs = (back, last, cos_t, sin_t)

        def job(number):
            p, corr = number // 2, number % 2 == 1
            source, target = (fg, corr_s) if corr else (fm, conv_s)
            s_ref, b_ref, t_ref = s_s.at[number], b_s.at[number], t_s.at[number]

            def product():
                for g in range(half // 8 + 1):
                    rows = slice(16 * g, 16 * g + 16)
                    k_re, k_im = fk[p, rows, :LANES].astype(F32), fk[p, rows, LANES:].astype(F32)
                    re = source[0, p, rows, :LANES].astype(F32)
                    im = source[0, p, rows, LANES:].astype(F32)
                    if corr:
                        s_ref[rows, :LANES] = (re * k_re + im * k_im).astype(LOW)
                        s_ref[rows, LANES:] = (im * k_re - re * k_im).astype(LOW)
                    else:
                        s_ref[rows, :LANES] = (re * k_re - im * k_im).astype(LOW)
                        s_ref[rows, LANES:] = (re * k_im + im * k_re).astype(LOW)

            def columns():
                inverse_columns(s_ref, tabs, b_ref)

            def twist():
                inverse_twist(tabs, b_ref, t_ref)

            def finish():
                y = inverse_rows(tabs, t_ref)
                for c in range(2):
                    channel = 2 * (step * together + p) + c
                    target[pl.ds(channel, half, stride=chans + 1), :] = y[
                        :, LANES * c : LANES * c + LANES
                    ]

            return product, columns, twist, finish

        staggered([job(number) for number in range(2 * together)])

    @pl.when(step >= steps)
    def _():
        chunk = step - steps
        token[...] = jnp.zeros_like(token)
        gain = jnp.broadcast_to(column(skip[...], chans), (chans, LANES))
        lane = lax.broadcasted_iota(jnp.int32, (chans, LANES), 1)
        row = lax.broadcasted_iota(jnp.int32, (chans, LANES), 0)
        inv = jnp.sum(
            jnp.where(lane == row + base_ref[0], lines[0:1, :], 0.0), axis=1, keepdims=True
        )
        inv = jnp.broadcast_to(inv, (chans, LANES))
        for a in range(chunk_rows):
            lanes = slice(LANES * a, LANES * a + LANES)
            rows = pl.ds((chunk * chunk_rows + a) * (chans + 1), chans)
            v = val[0, :, lanes].astype(F32)
            gi = gin[0, :, lanes].astype(F32)
            go = gout[0, :, lanes].astype(F32)
            co = cot[0, :, lanes].astype(F32)
            inner = inv * conv_s[rows, :] + gain * (gi * v)
            grad_mixed = inv * corr_s[rows, :] + gain * (co * go)
            gout_out[0, :, lanes] = (co * inner).astype(LOW)
            val_out[0, :, lanes] = (grad_mixed * gi).astype(LOW)
            gin_out[0, :, lanes] = (grad_mixed * v).astype(LOW)


INV_PI = 0.3183098861837907
PI_HIGH = 3.140625
PI_LOW = 9.676535897932795e-4


def fit(function, powers, top):
    nodes = np.cos(np.pi * (np.arange(400) + 0.5) / 800) * top
    design = np.stack([nodes**p for p in powers], axis=1)
    return [float(x) for x in np.linalg.lstsq(design, function(nodes), rcond=None)[0]]


SINE = fit(lambda x: np.sin(x) - x, (3, 5, 7, 9), np.pi / 2 + 1e-3)
COSINE = fit(lambda x: np.cos(x) - 1.0, (2, 4, 6, 8), np.pi / 2 + 1e-3)


def poly(coefficients, r2):
    p = coefficients[-1]
    for c in coefficients[-2::-1]:
        p = c + r2 * p
    return r2 * p


def sine_poly(r, r2):
    return r + r * poly(SINE, r2)


def cosine_poly(r2):
    return 1.0 + poly(COSINE, r2)


def sine_cosine(z):
    turns = jnp.floor(z * INV_PI + 0.5)
    r = (z - turns * PI_HIGH) - turns * PI_LOW
    halves = turns * 0.5
    sign = 1.0 - 4.0 * (halves - jnp.floor(halves))
    r2 = r * r
    return sign * sine_poly(r, r2), sign * cosine_poly(r2)


def column(row, size):
    lane = lax.broadcasted_iota(jnp.int32, (size, size), 1)
    diagonal = lane == lax.broadcasted_iota(jnp.int32, (size, size), 0)
    return jnp.sum(jnp.where(diagonal, row, 0.0), axis=1, keepdims=True)


def split(x):
    high = x.astype(LOW)
    return high, (x - high.astype(F32)).astype(LOW)


def triple_dot(weight, x):
    w_high, w_low = split(weight)
    x_high, x_low = split(x)
    wide = jnp.concatenate([w_high, w_high, w_low], axis=1)
    tall = jnp.concatenate([x_high, x_low, x_high], axis=0)
    return jnp.dot(wide, tall, preferred_element_type=F32)


def decay_tables(rates, start, channels, length):
    rate = column(rates, channels) * (-1.0 / length)
    lane = lax.broadcasted_iota(jnp.int32, (channels, LANES), 1)
    fine = jnp.exp(rate * lane.astype(F32))
    coarse = jnp.exp(rate * (start + LANES * lane).astype(F32))
    return fine, coarse


def filter_kernel(
    start_ref, freq, shift, w_in_t, b_in, w_mid, b_mid, w_out_t, rates,
    raw_out, feat_out, act_out, cos_out, w_in, w_out, *, length,
):
    width = feat_out.shape[1]
    order = w_mid.shape[1]
    channels = w_out_t.shape[1]

    @pl.when(pl.program_id(0) == 0)
    def _():
        w_in[...] = jnp.zeros_like(w_in)
        w_in[:, : w_in_t.shape[0]] = w_in_t[...].T
        w_out[...] = w_out_t[...].T

    start = start_ref[3] + pl.program_id(0) * width
    rows = freq.shape[0]
    position = start + lax.broadcasted_iota(jnp.int32, (rows, width), 1)
    freq_w = jnp.concatenate([freq[...]] * (width // LANES), axis=1)
    shift_w = jnp.concatenate([shift[...]] * (width // LANES), axis=1)
    quarter = length // 4
    phase = position * freq_w + shift_w
    sign = (1 - ((phase >> int(math.log2(length // 2))) & 1) * 2).astype(F32)
    angle = ((phase & (length // 2 - 1)) - quarter).astype(F32) * (2.0 * math.pi / length)
    wave = sign * sine_poly(angle, angle * angle)
    linear = lax.broadcasted_iota(jnp.int32, (rows, width), 0) == 0
    feature = jnp.where(linear, position.astype(F32) * (1.0 / length), wave)
    feat_out[...] = feature.astype(LOW)

    def layer(weight, x, bias, number):
        z = triple_dot(weight, x) + column(bias, order)
        sine, cosine = sine_cosine(z)
        act_out[order * number : order * number + order, :] = sine.astype(LOW)
        cos_out[order * number : order * number + order, :] = cosine.astype(LOW)
        return sine

    hidden = layer(w_in[...], feature, b_in[...], 0)
    hidden = layer(w_mid[0], hidden, b_mid[0:1, :], 1)
    hidden = layer(w_mid[1], hidden, b_mid[1:2, :], 2)
    shaped = triple_dot(w_out[...], hidden)
    fine, coarse = decay_tables(rates[...], start, channels, length)
    for a in range(width // LANES):
        decay = fine * coarse[:, a : a + 1]
        raw_out[:, a, :] = shaped[:, LANES * a : LANES * a + LANES] * decay


def nt_dot(x, y):
    return lax.dot_general(x, y, (((1,), (1,)), ((), ())), preferred_element_type=F32)


def filter_grad_kernel(
    start_ref, grad, feat, act, cosines, w_mid, w_out_t, rates, lines, skip_row, token,
    packed, d_out, d_mid, d_in, d_bias, *, length,
):
    step = pl.program_id(0)
    width = feat.shape[1]
    order = w_mid.shape[1]
    channels = w_out_t.shape[1]
    start = start_ref[3] + step * width

    @pl.when(step == 0)
    def _():
        for ref in (d_out, d_mid, d_in, d_bias):
            ref[...] = jnp.zeros_like(ref)

    fine, coarse = decay_tables(rates[...], start, channels, length)
    parts = [grad[:, a, :] * (fine * coarse[:, a : a + 1]) for a in range(width // LANES)]
    d_shaped = jnp.concatenate(parts, axis=1)

    def part(ref, number):
        return ref[order * number : order * number + order, :]

    def bias_sum(x, number):
        total = x[:, :LANES]
        for a in range(1, width // LANES):
            total = total + x[:, LANES * a : LANES * a + LANES]
        d_bias[number] = d_bias[number] + total

    d_out[...] = d_out[...] + nt_dot(d_shaped.astype(LOW), part(act, 2))
    dz = triple_dot(w_out_t[...], d_shaped) * part(cosines, 2)
    bias_sum(dz, 2)
    d_mid[1] = d_mid[1] + nt_dot(dz.astype(LOW), part(act, 1))
    dz = triple_dot(w_mid[1].T, dz) * part(cosines, 1)
    bias_sum(dz, 1)
    d_mid[0] = d_mid[0] + nt_dot(dz.astype(LOW), part(act, 0))
    dz = triple_dot(w_mid[0].T, dz) * part(cosines, 0)
    bias_sum(dz, 0)
    d_in[...] = d_in[...] + nt_dot(dz.astype(LOW), feat[...])

    @pl.when(step == pl.num_programs(0) - 1)
    def _():
        packed[...] = jnp.zeros_like(packed)
        packed[:channels, :order] = d_out[...]
        packed[:order, order : 2 * order] = d_mid[0]
        packed[order : 2 * order, order : 2 * order] = d_mid[1]
        base = channels
        features = d_in.shape[1]
        packed[base : base + order, :features] = d_in[...]
        spot = lax.broadcasted_iota(jnp.int32, (order, LANES), 1)
        current = packed[base : base + order, :]
        for number in range(3):
            total = jnp.sum(d_bias[number], axis=1, keepdims=True)
            current = jnp.where(spot == features + number, total, current)
        packed[base : base + order, :] = current
        base += order
        packed[base : base + 1, :] = lines[1:2, :]
        packed[base + 1 : base + 2, :] = skip_row[0:1, :]


def unpack_kernel(
    base_ref, own, other, w_in_t, b_in, w_mid, b_mid, w_out_t, rate, skip, whole,
    *, scale, features,
):
    size = own.shape[0]
    bit = base_ref[2]
    whole[pl.ds(pl.multiple_of(bit * size, 8), size), :] = own[...] * scale
    whole[pl.ds(pl.multiple_of((1 - bit) * size, 8), size), :] = other[...] * scale
    order, channels = w_out_t.shape
    w_out_t[...] = whole[:channels, :].T[:order, :]
    mid = whole[: 2 * order, order : 2 * order]
    w_mid[0] = mid[:order]
    w_mid[1] = mid[order:]
    base = channels
    block = whole[base : base + order, :]
    w_in_t[...] = block.T[: w_in_t.shape[0], :]
    lane = lax.broadcasted_iota(jnp.int32, (order, LANES), 1)
    row = lax.broadcasted_iota(jnp.int32, (order, LANES), 0)

    def as_row(number):
        values = jnp.sum(jnp.where(lane == features + number, block, 0.0), axis=1, keepdims=True)
        return jnp.sum(jnp.where(lane == row, values, 0.0), axis=0, keepdims=True)[:, :order]

    b_in[...] = as_row(0)
    b_mid[0:1, :] = as_row(1)
    b_mid[1:2, :] = as_row(2)
    base += order
    rate[...] = whole[base : base + 1, :channels]
    chans = skip.shape[1]
    skips = whole[base + 1 : base + 2, :]
    lane = lax.broadcasted_iota(jnp.int32, (chans, LANES), 1)
    row = lax.broadcasted_iota(jnp.int32, (chans, LANES), 0)
    values = jnp.sum(jnp.where(lane == row + base_ref[0], skips, 0.0), axis=1, keepdims=True)
    skip[...] = jnp.sum(jnp.where(lane == row, values, 0.0), axis=0, keepdims=True)[:, :chans]


def const_spec(array):
    zeros = (0,) * len(array.shape)
    return pl.BlockSpec(array.shape, lambda i: zeros)


SCALAR = pl.BlockSpec(memory_space=pltpu.SMEM)


def vmem(shape, dtype=F32):
    return pltpu.VMEM(shape, dtype)


def shape(dims, dtype=F32):
    return jax.ShapeDtypeStruct(dims, dtype)


def exchange(x, axis, bit):
    size = lax.axis_size(axis)
    return lax.ppermute(x, axis, [(s, s ^ bit) for s in range(size)])


def butterfly(x, axis, first=1):
    bit = first
    while bit < lax.axis_size(axis):
        x = x + exchange(x, axis, bit)
        bit *= 2
    return x


def local(
    value, gate_in, gate_out, cotangent, skip_gain,
    weight_in, bias_in, weight_mid, bias_mid, weight_out, decay_rate,
):
    seqs, chans, length = value.shape
    channels, order = weight_out.shape
    chan_count = lax.axis_size("chan")
    seq_count = lax.axis_size("seq")
    block = length // chan_count
    block_rows = block // LANES
    half = length // LANES
    pairs = chans // 2
    spec_rows = 2 * (half + 8)
    chunks = 4
    member = lax.axis_index("chan").astype(jnp.int32)
    base = jnp.stack([member * chans, member, member % 2, member * block])
    first, ahead, back, last, cos_t, sin_t = [jnp.asarray(t) for t in dft_tables(length)]
    feature_rows = 48
    bands = (weight_in.shape[1] - 1) // 2
    freq, shift = [jnp.asarray(t) for t in feature_tables(length, bands, feature_rows)]

    width = min(1024, block)
    steps = block // width
    rates = decay_rate.reshape(1, channels)
    w_out_t = weight_out.T
    w_in_t = weight_in.T
    weights = (w_in_t, bias_in.reshape(1, order), weight_mid, bias_mid, w_out_t, rates)
    raw_block, feats, acts, cosines = pl.pallas_call(
        functools.partial(filter_kernel, length=length),
        grid=(steps,),
        in_specs=[SCALAR] + [const_spec(x) for x in (freq, shift) + weights],
        out_specs=[
            pl.BlockSpec((channels, width // LANES, LANES), lambda i: (0, i, 0)),
            pl.BlockSpec((feature_rows, width), lambda i: (0, i)),
            pl.BlockSpec((3 * order, width), lambda i: (0, i)),
            pl.BlockSpec((3 * order, width), lambda i: (0, i)),
        ],
        out_shape=[
            shape((channels, block_rows, LANES)),
            shape((feature_rows, block), LOW),
            shape((3 * order, block), LOW),
            shape((3 * order, block), LOW),
        ],
        scratch_shapes=[vmem((order, feature_rows)), vmem((channels, order))],
        name="filter_rows",
    )(base, freq, shift, *weights)
    raw = lax.all_to_all(
        raw_block.reshape(chan_count, chans, block_rows, LANES),
        "chan", split_axis=0, concat_axis=0, tiled=True,
    )

    chunk = length // chunks
    tables = (first, ahead, back, last, cos_t, sin_t)
    early = lambda i: (0, 0, jnp.minimum(i, chunks - 1))
    late = lambda i: (0, jnp.maximum(i - chunks, 0), 0, 0)
    piece = lambda i: (0, jnp.maximum(i - chunks, 0), 0, 0)
    fm, fg, skip_row, grad_kernel = pl.pallas_call(
        functools.partial(
            spectra_kernel, chunks=chunks, seqs=seqs, chans=chans
        ),
        grid=(chunks + pairs,),
        in_specs=[SCALAR]
        + [pl.BlockSpec((seqs, chans, chunk), early)] * 4
        + [const_spec(x) for x in tables],
        out_specs=[
            pl.BlockSpec((seqs, 1, spec_rows, 2 * LANES), late),
            pl.BlockSpec((seqs, 1, spec_rows, 2 * LANES), late),
            pl.BlockSpec((8, LANES), lambda i: (0, 0)),
        ]
        + [pl.BlockSpec((chan_count, 2, block_rows, LANES), piece)],
        out_shape=[
            shape((seqs, pairs, spec_rows, 2 * LANES), LOW),
            shape((seqs, pairs, spec_rows, 2 * LANES), LOW),
            shape((8, LANES)),
        ]
        + [shape((chan_count, chans, block_rows, LANES))],
        scratch_shapes=[
            vmem((seqs, half * (chans + 1), LANES)),
            vmem((seqs, half * (chans + 1), LANES)),
            vmem((chans, LANES)),
            vmem((2 * seqs, 2 * half, 2 * LANES)),
            vmem((2 * seqs, spec_rows, 2 * LANES), LOW),
            vmem((2 * seqs, spec_rows, 2 * LANES)),
            vmem((spec_rows, 2 * LANES), LOW),
            vmem((spec_rows, 2 * LANES)),
            vmem((2 * half, 2 * LANES), LOW),
        ],
        name="spectra",
    )(base, value, gate_in, gate_out, cotangent, *tables)

    ahead_tabs = (first, ahead, cos_t, sin_t)
    together = 2 if pairs % 2 == 0 else 1
    group = 2 * together
    fk, grad_raw, lines = pl.pallas_call(
        functools.partial(kernel_kernel, length=length),
        grid=(pairs // together,),
        in_specs=[
            SCALAR,
            pl.BlockSpec((chan_count, group, block_rows, LANES), lambda i: (0, i, 0, 0)),
            pl.BlockSpec((chan_count, group, block_rows, LANES), lambda i: (0, i, 0, 0)),
        ]
        + [const_spec(x) for x in ahead_tabs],
        out_specs=[
            pl.BlockSpec((together, spec_rows, 2 * LANES), lambda i: (i, 0, 0)),
            pl.BlockSpec((chan_count, group, block_rows, LANES), lambda i: (0, i, 0, 0)),
            pl.BlockSpec((8, LANES), lambda i: (0, 0)),
        ],
        out_shape=[
            shape((pairs, spec_rows, 2 * LANES), LOW),
            shape((chan_count, chans, block_rows, LANES)),
            shape((8, LANES)),
        ],
        scratch_shapes=[
            vmem((together, 2 * half, 2 * LANES)),
            vmem((together, spec_rows, 2 * LANES), LOW),
        ],
        name="filter_spectrum",
    )(base, raw, grad_kernel, *ahead_tabs)
    taken = lax.all_to_all(grad_raw, "chan", split_axis=0, concat_axis=0, tiled=True)

    back_tabs = (back, last, cos_t, sin_t)
    skip_line = skip_gain.reshape(1, chans)
    anywhere = pl.BlockSpec(memory_space=pl.ANY)
    out_steps = pairs // together

    def outputs(b, after, held):
        early4 = lambda i: (b, jnp.minimum(i, out_steps - 1), 0, 0)
        early3 = lambda i: (jnp.minimum(i, out_steps - 1), 0, 0)
        late3 = lambda i: (b, 0, jnp.maximum(i - out_steps, 0))
        signal_spec = pl.BlockSpec((1, chans, chunk), late3)
        wide_spec = pl.BlockSpec((1, together, spec_rows, 2 * LANES), early4)
        operands = (
            base, fm, fg, fk, value, gate_in, gate_out, cotangent, skip_line, lines,
        ) + back_tabs
        extras = tuple(after) + tuple(held)
        return pl.pallas_call(
            functools.partial(output_kernel, steps=out_steps, chunks=chunks, chans=chans),
            grid=(out_steps + chunks,),
            in_specs=[SCALAR, wide_spec, wide_spec]
            + [pl.BlockSpec((together, spec_rows, 2 * LANES), early3)]
            + [signal_spec] * 4
            + [const_spec(x) for x in (skip_line, lines) + back_tabs]
            + [anywhere] * len(extras),
            out_specs=[signal_spec] * 3 + [pl.BlockSpec((8, LANES), lambda i: (0, 0))],
            out_shape=[shape((seqs, chans, length), LOW)] * 3 + [shape((8, LANES))],
            input_output_aliases={
                len(operands) + len(after) + n: n for n in range(len(held))
            },
            scratch_shapes=[
                vmem((half * (chans + 1), LANES)),
                vmem((half * (chans + 1), LANES)),
                vmem((2 * together, spec_rows, 2 * LANES), LOW),
                vmem((2 * together, spec_rows, 2 * LANES)),
                vmem((2 * together, 2 * half, 2 * LANES), LOW),
            ],
            name="outputs",
        )(*operands, *extras)

    early_count = seqs
    held, token = (), lines
    for b in range(early_count):
        *held, token = outputs(b, (), held)

    packed_rows = -(-(channels + order + 2) // 16) * 16
    wide_spec = lambda rows: pl.BlockSpec((rows, width // LANES, LANES), lambda i: (0, i, 0))
    packed = pl.pallas_call(
        functools.partial(filter_grad_kernel, length=length),
        grid=(steps,),
        in_specs=[
            SCALAR,
            wide_spec(channels),
            pl.BlockSpec((feature_rows, width), lambda i: (0, i)),
            pl.BlockSpec((3 * order, width), lambda i: (0, i)),
            pl.BlockSpec((3 * order, width), lambda i: (0, i)),
        ]
        + [const_spec(x) for x in (weight_mid, w_out_t, rates, lines, skip_row)]
        + [anywhere],
        out_specs=pl.BlockSpec((packed_rows, LANES), lambda i: (0, 0)),
        out_shape=shape((packed_rows, LANES)),
        scratch_shapes=[
            vmem((channels, order)),
            vmem((2, order, order)),
            vmem((order, feature_rows)),
            vmem((3, order, LANES)),
        ],
        name="filter_gradients",
    )(
        base, taken.reshape(channels, block_rows, LANES), feats, acts, cosines, weight_mid,
        w_out_t, rates, lines, skip_row, token,
    )
    for b in range(early_count, seqs):
        *held, token = outputs(b, (packed,), held)
    grad_val, grad_gin, grad_gout = held

    halves = packed.reshape(2, packed_rows // 2, LANES)
    keep = jnp.where(member % 2 == 0, halves[0], halves[1])
    give = jnp.where(member % 2 == 0, halves[1], halves[0])
    own = butterfly(keep + exchange(give, "chan", 1), "chan", 2)
    own = butterfly(own, "seq")
    other = exchange(own, "chan", 1)
    factor = 1.0 / math.sqrt(seqs * seq_count * length)
    d_in_t, d_bin, d_mid, d_bmid, d_out_t, d_rate, d_skip = pl.pallas_call(
        functools.partial(unpack_kernel, scale=factor, features=feature_rows),
        in_specs=[SCALAR, pl.BlockSpec(), pl.BlockSpec()],
        out_shape=[
            shape(weight_in.shape[::-1]),
            shape((1, order)),
            shape(weight_mid.shape),
            shape(bias_mid.shape),
            shape(weight_out.shape[::-1]),
            shape((1, channels)),
            shape((1, chans)),
        ],
        scratch_shapes=[vmem((packed_rows, LANES))],
        name="unpack",
    )(base, own, other)
    return (
        grad_val, grad_gin, grad_gout, d_skip[0],
        d_in_t.T, d_bin[0], d_mid, d_bmid, d_out_t.T, d_rate[0],
    )


def solution(mesh):
    large = P("seq", "chan", None)
    return jax.shard_map(
        local,
        mesh=mesh,
        in_specs=(large,) * 4 + (P("chan"),) + (P(),) * 6,
        out_specs=(large,) * 3 + (P("chan"),) + (P(),) * 6,
        check_vma=False,
    )
```

```python
import functools
import math

import jax
import jax.numpy as jnp
import numpy as np
from jax import lax
from jax.experimental import pallas as pl
from jax.experimental.pallas import tpu as pltpu
from jax.sharding import PartitionSpec as P

EPSILON = 1e-06
LANES = 128
F32 = jnp.float32
LOW = jnp.bfloat16


def band_table(length, bands):
    highest = length / 4.0
    return np.array(
        [math.floor(highest ** (number / (bands - 1)) + 0.5) for number in range(bands)], np.int32
    )


def feature_tables(length, bands, rows):
    freq = np.zeros((rows, LANES), np.int32)
    shift = np.full((rows, LANES), length // 4, np.int32)
    table = band_table(length, bands)[:, None]
    freq[1 : 1 + bands] = table
    shift[1 : 1 + bands] = length // 2
    freq[1 + bands : 1 + 2 * bands] = table
    return freq, shift


def dft_tables(length):
    half = length // LANES
    rows = 2 * half
    k = np.arange(half)[:, None]
    a = np.arange(half)[None, :]
    angle = 2.0 * np.pi / rows * (k * a % rows)
    cos_rows = np.cos(angle)
    sin_rows = np.sin(angle)
    alternating = 1.0 - 2.0 * (np.arange(half) % 2)
    first = np.concatenate([cos_rows, -sin_rows], axis=0)
    first[half] = alternating
    weight = np.full((half, 1), 2.0)
    weight[0] = 1.0
    last = np.concatenate([cos_rows * weight, -sin_rows * weight], axis=0)
    last[half] = alternating
    last = last.T / (2.0 * length)
    col = np.arange(LANES)
    angle = 2.0 * np.pi / LANES * (col[:, None] * col[None, :] % LANES)
    cos_cols, sin_cols = np.cos(angle), np.sin(angle)
    ahead = np.block([[cos_cols, -sin_cols], [sin_cols, cos_cols]])
    back = np.block([[cos_cols, sin_cols], [-sin_cols, cos_cols]])
    total = 2 * length
    twist_rows = np.arange(half + 8)[:, None]
    angle = 2.0 * np.pi / total * (twist_rows * col[None, :] % total)
    low = lambda x: x.astype(np.float32).astype(LOW)
    return (
        low(first),
        low(ahead),
        low(back),
        low(last),
        np.cos(angle).astype(np.float32),
        np.sin(angle).astype(np.float32),
    )


def forward_rows(signal, tabs, r_ref):
    r_ref[...] = jnp.dot(tabs[0][...], signal, preferred_element_type=F32)


def forward_columns(tabs, h_ref):
    return jnp.dot(h_ref[...], tabs[1][...], preferred_element_type=F32)


def forward_pair(signal, tabs, r_ref, h_ref):
    forward_rows(signal, tabs, r_ref)
    forward_twist(tabs, r_ref, h_ref)
    return forward_columns(tabs, h_ref)


def forward_twist(tabs, r_ref, h_ref):
    first, ahead, cos_t, sin_t = tabs
    half = first.shape[1]
    groups = half // 8
    top = lax.broadcasted_iota(jnp.int32, (8, LANES), 0) == 0
    for g in range(groups + 1):
        cosine = cos_t[8 * g : 8 * g + 8, :]
        sine = sin_t[8 * g : 8 * g + 8, :]
        real, imag = [], []
        for c in range(2):
            lanes = slice(LANES * c, LANES * c + LANES)
            if g < groups:
                g_re = r_ref[8 * g : 8 * g + 8, lanes]
                g_im = r_ref[half + 8 * g : half + 8 * g + 8, lanes]
                if g == 0:
                    g_im = jnp.where(top, 0.0, g_im)
                real.append(g_re * cosine + g_im * sine)
                imag.append(g_im * cosine - g_re * sine)
            else:
                g_re = jnp.where(top, r_ref[half : half + 8, lanes], 0.0)
                real.append(g_re * cosine)
                imag.append(-(g_re * sine))
        rows = slice(16 * g, 16 * g + 16)
        h_ref[rows, :LANES] = jnp.concatenate(real, axis=0).astype(LOW)
        h_ref[rows, LANES:] = jnp.concatenate(imag, axis=0).astype(LOW)


def inverse_columns(s_ref, tabs, b_ref):
    b_ref[...] = jnp.dot(s_ref[...], tabs[0][...], preferred_element_type=F32)


def inverse_twist(tabs, b_ref, t_ref):
    _, last, cos_t, sin_t = tabs
    half = last.shape[0]
    groups = half // 8
    top = lax.broadcasted_iota(jnp.int32, (8, LANES), 0) == 0

    def turned(g, c):
        rows = slice(16 * g + 8 * c, 16 * g + 8 * c + 8)
        re, im = b_ref[rows, :LANES], b_ref[rows, LANES:]
        cosine = cos_t[8 * g : 8 * g + 8, :]
        sine = sin_t[8 * g : 8 * g + 8, :]
        return re * cosine - im * sine, re * sine + im * cosine

    for g in range(0, groups, 2):
        for c in range(2):
            lanes = slice(LANES * c, LANES * c + LANES)
            re0, im0 = turned(g, c)
            re1, im1 = turned(g + 1, c)
            if g == 0:
                im0 = jnp.where(top, turned(groups, c)[0], im0)
            t_ref[8 * g : 8 * g + 16, lanes] = jnp.concatenate([re0, re1], axis=0).astype(LOW)
            t_ref[half + 8 * g : half + 8 * g + 16, lanes] = jnp.concatenate(
                [im0, im1], axis=0
            ).astype(LOW)


def inverse_rows(tabs, t_ref):
    return jnp.dot(tabs[1][...], t_ref[...], preferred_element_type=F32)


def inverse_pair(s_ref, tabs, b_ref, t_ref):
    inverse_columns(s_ref, tabs, b_ref)
    inverse_twist(tabs, b_ref, t_ref)
    return inverse_rows(tabs, t_ref)


def staggered(jobs):
    stages = max(len(job) for job in jobs)
    for when in range(len(jobs) + stages - 1):
        for number in reversed(range(len(jobs))):
            stage = when - number
            if 0 <= stage < len(jobs[number]):
                jobs[number][stage]()


def spectra_kernel(
    base_ref, val, gin, gout, cot, first, ahead, back, last, cos_t, sin_t,
    fm_out, fg_out, skip_out, grad_out,
    mix_s, grad_s, skip_s, r_s, h_s, f_s, cross_s, b_s, t_s, *, chunks, seqs, chans,
):
    step = pl.program_id(0)
    chunk_rows = val.shape[2] // LANES
    half = chunk_rows * chunks

    @pl.when(step == 0)
    def _():
        skip_s[...] = jnp.zeros_like(skip_s)

    @pl.when(step < chunks)
    def _():
        for b in range(seqs):
            total = skip_s[...]
            for a in range(chunk_rows):
                lanes = slice(LANES * a, LANES * a + LANES)
                mixed = gin[b, :, lanes].astype(F32) * val[b, :, lanes].astype(F32)
                inner = cot[b, :, lanes].astype(F32) * gout[b, :, lanes].astype(F32)
                rows = pl.ds((step * chunk_rows + a) * (chans + 1), chans)
                mix_s[b, rows, :] = mixed
                grad_s[b, rows, :] = inner
                total = total + mixed * inner
            skip_s[...] = total

    @pl.when(step == chunks - 1)
    def _():
        per_row = jnp.sum(skip_s[...], axis=1, keepdims=True)
        lane = lax.broadcasted_iota(jnp.int32, (chans, LANES), 1)
        row = lax.broadcasted_iota(jnp.int32, (chans, LANES), 0)
        mine = lane == row + base_ref[0]
        spread = jnp.sum(jnp.where(mine, per_row, 0.0), axis=0, keepdims=True)
        top = lax.broadcasted_iota(jnp.int32, (8, LANES), 0) == 0
        skip_out[...] = jnp.where(top, spread, 0.0)

    @pl.when(step >= chunks)
    def _():
        pair = step - chunks
        tabs = (first, ahead, cos_t, sin_t)

        def job(number):
            b, inner = number // 2, number % 2 == 1
            source, target = (grad_s, fg_out) if inner else (mix_s, fm_out)
            r_ref, h_ref = r_s.at[number], h_s.at[number]

            def rows():
                parts = [
                    source[b, pl.ds(2 * pair + c, half, stride=chans + 1), :] for c in range(2)
                ]
                forward_rows(jnp.concatenate(parts, axis=1).astype(LOW), tabs, r_ref)

            def twist():
                forward_twist(tabs, r_ref, h_ref)

            def columns():
                f_s[number] = forward_columns(tabs, h_ref)
                target[b, 0] = f_s[number].astype(LOW)

            return rows, twist, columns

        staggered([job(number) for number in range(2 * seqs)])
        for g in range(half // 8 + 1):
            rows = slice(16 * g, 16 * g + 16)
            cross_re = cross_im = None
            for b in range(seqs):
                m_re, m_im = f_s[2 * b, rows, :LANES], f_s[2 * b, rows, LANES:]
                g_re, g_im = f_s[2 * b + 1, rows, :LANES], f_s[2 * b + 1, rows, LANES:]
                c_re = m_re * g_re + m_im * g_im
                c_im = m_re * g_im - m_im * g_re
                cross_re = c_re if b == 0 else cross_re + c_re
                cross_im = c_im if b == 0 else cross_im + c_im
            cross_s[rows, :LANES] = cross_re.astype(LOW)
            cross_s[rows, LANES:] = cross_im.astype(LOW)
        y = inverse_pair(cross_s, (back, last, cos_t, sin_t), b_s, t_s)
        members, _, each, _ = grad_out.shape
        for c in range(2):
            lanes = slice(LANES * c, LANES * c + LANES)
            grad_out[:, c] = y[:, lanes].reshape(members, each, LANES)


def norm_kernel(base_ref, raw, grads, after, grad_out, lines_out, *, length):
    step = pl.program_id(0)
    blocks, channels, rows_each, _ = raw.shape
    half = blocks * rows_each
    lane = lax.broadcasted_iota(jnp.int32, (8, LANES), 1)
    line = lax.broadcasted_iota(jnp.int32, (8, LANES), 0)
    position = (
        lax.broadcasted_iota(jnp.int32, (half, LANES), 0) * LANES
        + lax.broadcasted_iota(jnp.int32, (half, LANES), 1)
    ).astype(F32) * (-1.0 / length)

    @pl.when(step == 0)
    def _():
        lines_out[...] = jnp.zeros_like(lines_out)

    total = lines_out[...]
    for c in range(channels):
        row, grad = raw[:, c].reshape(half, LANES), grads[:, c].reshape(half, LANES)
        square_rows, cross_rows = row * row, row * grad
        square = jnp.sum(square_rows, keepdims=True) + EPSILON
        inv = 1.0 / jnp.sqrt(square)
        coef = jnp.sum(cross_rows, keepdims=True) * (inv / square)
        rate = inv * jnp.sum(cross_rows * position, keepdims=True) - coef * jnp.sum(
            square_rows * position, keepdims=True
        )
        grad_out[:, c] = (grad * inv - row * coef).reshape(blocks, rows_each, LANES)
        mine = lane == base_ref[0] + channels * step + c
        for number, x in enumerate((inv, rate)):
            total = jnp.where(jnp.logical_and(mine, line == number), x, total)
    lines_out[...] = total


def kernel_kernel(raw, after, first, ahead, cos_t, sin_t, fk_out, r_s, h_s):
    blocks, channels, rows_each, _ = raw.shape
    half = blocks * rows_each
    tabs = (first, ahead, cos_t, sin_t)

    def job(number):
        def rows():
            parts = [raw[:, 2 * number + c].reshape(half, LANES) for c in range(2)]
            signal = jnp.concatenate(parts, axis=1).astype(LOW)
            forward_rows(signal, tabs, r_s.at[number])

        def twist():
            forward_twist(tabs, r_s.at[number], h_s.at[number])

        def columns():
            fk_out[number] = forward_columns(tabs, h_s.at[number]).astype(LOW)

        return rows, twist, columns

    staggered([job(number) for number in range(channels // 2)])


def output_kernel(
    base_ref, fm, fg, fk, val, gin, gout, cot, skip, lines, back, last, cos_t, sin_t, *rest,
    steps, chunks, chans,
):
    val_out, gin_out, gout_out, token, conv_s, corr_s, s_s, b_s, t_s = rest[-9:]
    step = pl.program_id(0)
    chunk_rows = val.shape[2] // LANES
    half = chunk_rows * chunks
    together = fk.shape[0]

    @pl.when(step < steps)
    def _():
        tabs = (back, last, cos_t, sin_t)

        height = 2 * (half + 8)

        def job(p):
            s_ref, b_ref, t_ref = s_s.at[p], b_s.at[p], t_s.at[p]

            def product():
                for g in range(half // 8 + 1):
                    rows = slice(16 * g, 16 * g + 16)
                    lower = slice(height + 16 * g, height + 16 * g + 16)
                    k_re, k_im = fk[p, rows, :LANES].astype(F32), fk[p, rows, LANES:].astype(F32)
                    re, im = fm[0, p, rows, :LANES].astype(F32), fm[0, p, rows, LANES:].astype(F32)
                    s_ref[rows, :LANES] = (re * k_re - im * k_im).astype(LOW)
                    s_ref[rows, LANES:] = (re * k_im + im * k_re).astype(LOW)
                    re, im = fg[0, p, rows, :LANES].astype(F32), fg[0, p, rows, LANES:].astype(F32)
                    s_ref[lower, :LANES] = (re * k_re + im * k_im).astype(LOW)
                    s_ref[lower, LANES:] = (im * k_re - re * k_im).astype(LOW)

            def columns():
                inverse_columns(s_ref, tabs, b_ref)

            def twist():
                for number in range(2):
                    inverse_twist(
                        tabs,
                        b_ref.at[height * number : height * number + height],
                        t_ref.at[:, 2 * LANES * number : 2 * LANES * number + 2 * LANES],
                    )

            def finish():
                y = inverse_rows(tabs, t_ref)
                for number, target in enumerate((conv_s, corr_s)):
                    for c in range(2):
                        channel = 2 * (step * together + p) + c
                        lanes = LANES * (2 * number + c)
                        target[pl.ds(channel, half, stride=chans + 1), :] = y[
                            :, lanes : lanes + LANES
                        ]

            return product, columns, twist, finish

        staggered([job(p) for p in range(together)])

    @pl.when(step >= steps)
    def _():
        chunk = step - steps
        token[...] = jnp.zeros_like(token)
        gain = jnp.broadcast_to(column(skip[...], chans), (chans, LANES))
        lane = lax.broadcasted_iota(jnp.int32, (chans, LANES), 1)
        row = lax.broadcasted_iota(jnp.int32, (chans, LANES), 0)
        inv = jnp.sum(
            jnp.where(lane == row + base_ref[0], lines[0:1, :], 0.0), axis=1, keepdims=True
        )
        inv = jnp.broadcast_to(inv, (chans, LANES))
        for a in range(chunk_rows):
            lanes = slice(LANES * a, LANES * a + LANES)
            rows = pl.ds((chunk * chunk_rows + a) * (chans + 1), chans)
            v = val[0, :, lanes].astype(F32)
            gi = gin[0, :, lanes].astype(F32)
            go = gout[0, :, lanes].astype(F32)
            co = cot[0, :, lanes].astype(F32)
            inner = inv * conv_s[rows, :] + gain * (gi * v)
            grad_mixed = inv * corr_s[rows, :] + gain * (co * go)
            gout_out[0, :, lanes] = (co * inner).astype(LOW)
            val_out[0, :, lanes] = (grad_mixed * gi).astype(LOW)
            gin_out[0, :, lanes] = (grad_mixed * v).astype(LOW)


INV_PI = 0.3183098861837907
PI_HIGH = 3.140625
PI_LOW = 9.676535897932795e-4


def fit(function, powers, top):
    nodes = np.cos(np.pi * (np.arange(400) + 0.5) / 800) * top
    design = np.stack([nodes**p for p in powers], axis=1)
    return [float(x) for x in np.linalg.lstsq(design, function(nodes), rcond=None)[0]]


SINE = fit(lambda x: np.sin(x) - x, (3, 5, 7, 9), np.pi / 2 + 1e-3)
COSINE = fit(lambda x: np.cos(x) - 1.0, (2, 4, 6, 8), np.pi / 2 + 1e-3)


def poly(coefficients, r2):
    p = coefficients[-1]
    for c in coefficients[-2::-1]:
        p = c + r2 * p
    return r2 * p


def sine_poly(r, r2):
    return r + r * poly(SINE, r2)


def cosine_poly(r2):
    return 1.0 + poly(COSINE, r2)


def sine_cosine(z):
    turns = jnp.floor(z * INV_PI + 0.5)
    r = (z - turns * PI_HIGH) - turns * PI_LOW
    halves = turns * 0.5
    sign = 1.0 - 4.0 * (halves - jnp.floor(halves))
    r2 = r * r
    return sign * sine_poly(r, r2), sign * cosine_poly(r2)


def column(row, size):
    lane = lax.broadcasted_iota(jnp.int32, (size, size), 1)
    diagonal = lane == lax.broadcasted_iota(jnp.int32, (size, size), 0)
    return jnp.sum(jnp.where(diagonal, row, 0.0), axis=1, keepdims=True)


def split(x):
    high = x.astype(LOW)
    return high, (x - high.astype(F32)).astype(LOW)


def triple_dot(weight, x):
    w_high, w_low = split(weight)
    x_high, x_low = split(x)
    wide = jnp.concatenate([w_high, w_high, w_low], axis=1)
    tall = jnp.concatenate([x_high, x_low, x_high], axis=0)
    return jnp.dot(wide, tall, preferred_element_type=F32)


def decay_tables(rates, start, channels, length):
    rate = column(rates, channels) * (-1.0 / length)
    lane = lax.broadcasted_iota(jnp.int32, (channels, LANES), 1)
    fine = jnp.exp(rate * lane.astype(F32))
    coarse = jnp.exp(rate * (start + LANES * lane).astype(F32))
    return fine, coarse


def sine(z):
    turns = jnp.floor(z * INV_PI + 0.5)
    r = (z - turns * PI_HIGH) - turns * PI_LOW
    halves = turns * 0.5
    sign = 1.0 - 4.0 * (halves - jnp.floor(halves))
    return sign * sine_poly(r, r * r)


def features(start, freq, shift, width, length):
    rows = freq.shape[0]
    position = start + lax.broadcasted_iota(jnp.int32, (rows, width), 1)
    freq_w = jnp.concatenate([freq[...]] * (width // LANES), axis=1)
    shift_w = jnp.concatenate([shift[...]] * (width // LANES), axis=1)
    quarter = length // 4
    phase = position * freq_w + shift_w
    sign = (1 - ((phase >> int(math.log2(length // 2))) & 1) * 2).astype(F32)
    angle = ((phase & (length // 2 - 1)) - quarter).astype(F32) * (2.0 * math.pi / length)
    wave = sign * sine_poly(angle, angle * angle)
    linear = lax.broadcasted_iota(jnp.int32, (rows, width), 0) == 0
    return jnp.where(linear, position.astype(F32) * (1.0 / length), wave)


def widen(w_in, w_in_t):
    w_in[...] = jnp.zeros_like(w_in)
    w_in[:, : w_in_t.shape[0]] = w_in_t[...].T


def filter_kernel(
    start_ref, freq, shift, w_in_t, b_in, w_mid, b_mid, w_out_t, rates,
    raw_out, w_in, w_out, *, length,
):
    width = raw_out.shape[1] * LANES
    order = w_mid.shape[1]
    channels = w_out_t.shape[1]

    @pl.when(pl.program_id(0) == 0)
    def _():
        widen(w_in, w_in_t)
        w_out[...] = w_out_t[...].T

    start = start_ref[3] + pl.program_id(0) * width
    hidden = features(start, freq, shift, width, length)
    weights = ((w_in[...], b_in[...]), (w_mid[0], b_mid[0:1, :]), (w_mid[1], b_mid[1:2, :]))
    for weight, bias in weights:
        hidden = sine(triple_dot(weight, hidden) + column(bias, order))
    shaped = triple_dot(w_out[...], hidden)
    fine, coarse = decay_tables(rates[...], start, channels, length)
    for a in range(width // LANES):
        decay = fine * coarse[:, a : a + 1]
        raw_out[:, a, :] = shaped[:, LANES * a : LANES * a + LANES] * decay


def activation_kernel(
    start_ref, freq, shift, w_in_t, b_in, w_mid, b_mid, after,
    feat_out, act_out, cos_out, w_in, *, length,
):
    width = feat_out.shape[1]
    order = w_mid.shape[1]

    @pl.when(pl.program_id(0) == 0)
    def _():
        widen(w_in, w_in_t)

    start = start_ref[3] + pl.program_id(0) * width
    hidden = features(start, freq, shift, width, length)
    feat_out[...] = hidden.astype(LOW)
    weights = ((w_in[...], b_in[...]), (w_mid[0], b_mid[0:1, :]), (w_mid[1], b_mid[1:2, :]))
    for number, (weight, bias) in enumerate(weights):
        z = triple_dot(weight, hidden) + column(bias, order)
        hidden, cosine = sine_cosine(z)
        rows = slice(order * number, order * number + order)
        act_out[rows, :] = hidden.astype(LOW)
        cos_out[rows, :] = cosine.astype(LOW)


def double_dot(weight, x):
    wide = jnp.concatenate(split(weight), axis=1)
    return jnp.dot(wide, jnp.concatenate([x, x], axis=0), preferred_element_type=F32)


def nt_dot(x, y):
    return lax.dot_general(x, y, (((1,), (1,)), ((), ())), preferred_element_type=F32)


def filter_grad_kernel(
    start_ref, grad, feat, act, cosines, w_mid, w_out_t, rates, lines, skip_row, token,
    packed, d_out, d_mid, d_in, d_bias, *, length,
):
    step = pl.program_id(0)
    width = feat.shape[1]
    order = w_mid.shape[1]
    channels = w_out_t.shape[1]
    start = start_ref[3] + step * width

    @pl.when(step == 0)
    def _():
        for ref in (d_out, d_mid, d_in, d_bias):
            ref[...] = jnp.zeros_like(ref)

    fine, coarse = decay_tables(rates[...], start, channels, length)
    parts = [grad[:, a, :] * (fine * coarse[:, a : a + 1]) for a in range(width // LANES)]
    d_shaped = jnp.concatenate(parts, axis=1)

    def part(ref, number):
        return ref[order * number : order * number + order, :]

    def bias_sum(x, number):
        total = x[:, :LANES]
        for a in range(1, width // LANES):
            total = total + x[:, LANES * a : LANES * a + LANES]
        d_bias[number] = d_bias[number] + total

    low = d_shaped.astype(LOW)
    d_out[...] = d_out[...] + nt_dot(low, part(act, 2))
    dz = double_dot(w_out_t[...], low) * part(cosines, 2).astype(F32)
    bias_sum(dz, 2)
    low = dz.astype(LOW)
    d_mid[1] = d_mid[1] + nt_dot(low, part(act, 1))
    dz = double_dot(w_mid[1].T, low) * part(cosines, 1).astype(F32)
    bias_sum(dz, 1)
    low = dz.astype(LOW)
    d_mid[0] = d_mid[0] + nt_dot(low, part(act, 0))
    dz = double_dot(w_mid[0].T, low) * part(cosines, 0).astype(F32)
    bias_sum(dz, 0)
    d_in[...] = d_in[...] + nt_dot(dz.astype(LOW), feat[...])

    @pl.when(step == pl.num_programs(0) - 1)
    def _():
        packed[...] = jnp.zeros_like(packed)
        packed[:channels, :order] = d_out[...]
        packed[:order, order : 2 * order] = d_mid[0]
        packed[order : 2 * order, order : 2 * order] = d_mid[1]
        base = channels
        features = d_in.shape[1]
        packed[base : base + order, :features] = d_in[...]
        spot = lax.broadcasted_iota(jnp.int32, (order, LANES), 1)
        current = packed[base : base + order, :]
        for number in range(3):
            total = jnp.sum(d_bias[number], axis=1, keepdims=True)
            current = jnp.where(spot == features + number, total, current)
        packed[base : base + order, :] = current
        base += order
        packed[base : base + 1, :] = lines[1:2, :]
        packed[base + 1 : base + 2, :] = skip_row[0:1, :]


def unpack_kernel(
    base_ref, own, other, w_in_t, b_in, w_mid, b_mid, w_out_t, rate, skip, whole,
    *, scale, features,
):
    size = own.shape[0]
    bit = base_ref[2]
    whole[pl.ds(pl.multiple_of(bit * size, 8), size), :] = own[...] * scale
    whole[pl.ds(pl.multiple_of((1 - bit) * size, 8), size), :] = other[...] * scale
    order, channels = w_out_t.shape
    w_out_t[...] = whole[:channels, :].T[:order, :]
    mid = whole[: 2 * order, order : 2 * order]
    w_mid[0] = mid[:order]
    w_mid[1] = mid[order:]
    base = channels
    block = whole[base : base + order, :]
    w_in_t[...] = block.T[: w_in_t.shape[0], :]
    lane = lax.broadcasted_iota(jnp.int32, (order, LANES), 1)
    row = lax.broadcasted_iota(jnp.int32, (order, LANES), 0)

    def as_row(number):
        values = jnp.sum(jnp.where(lane == features + number, block, 0.0), axis=1, keepdims=True)
        return jnp.sum(jnp.where(lane == row, values, 0.0), axis=0, keepdims=True)[:, :order]

    b_in[...] = as_row(0)
    b_mid[0:1, :] = as_row(1)
    b_mid[1:2, :] = as_row(2)
    base += order
    rate[...] = whole[base : base + 1, :channels]
    chans = skip.shape[1]
    skips = whole[base + 1 : base + 2, :]
    lane = lax.broadcasted_iota(jnp.int32, (chans, LANES), 1)
    row = lax.broadcasted_iota(jnp.int32, (chans, LANES), 0)
    values = jnp.sum(jnp.where(lane == row + base_ref[0], skips, 0.0), axis=1, keepdims=True)
    skip[...] = jnp.sum(jnp.where(lane == row, values, 0.0), axis=0, keepdims=True)[:, :chans]


def const_spec(array):
    zeros = (0,) * len(array.shape)
    return pl.BlockSpec(array.shape, lambda i: zeros)


SCALAR = pl.BlockSpec(memory_space=pltpu.SMEM)


def vmem(shape, dtype=F32):
    return pltpu.VMEM(shape, dtype)


def shape(dims, dtype=F32):
    return jax.ShapeDtypeStruct(dims, dtype)


def exchange(x, axis, bit):
    size = lax.axis_size(axis)
    return lax.ppermute(x, axis, [(s, s ^ bit) for s in range(size)])


def butterfly(x, axis, first=1):
    bit = first
    while bit < lax.axis_size(axis):
        x = x + exchange(x, axis, bit)
        bit *= 2
    return x


def local(
    value, gate_in, gate_out, cotangent, skip_gain,
    weight_in, bias_in, weight_mid, bias_mid, weight_out, decay_rate,
):
    seqs, chans, length = value.shape
    channels, order = weight_out.shape
    chan_count = lax.axis_size("chan")
    seq_count = lax.axis_size("seq")
    block = length // chan_count
    block_rows = block // LANES
    half = length // LANES
    pairs = chans // 2
    spec_rows = 2 * (half + 8)
    chunks = 4
    member = lax.axis_index("chan").astype(jnp.int32)
    base = jnp.stack([member * chans, member, member % 2, member * block])
    first, ahead, back, last, cos_t, sin_t = [jnp.asarray(t) for t in dft_tables(length)]
    feature_rows = 48
    bands = (weight_in.shape[1] - 1) // 2
    freq, shift = [jnp.asarray(t) for t in feature_tables(length, bands, feature_rows)]

    width = min(2048, block)
    steps = block // width
    rates = decay_rate.reshape(1, channels)
    w_out_t = weight_out.T
    w_in_t = weight_in.T
    weights = (w_in_t, bias_in.reshape(1, order), weight_mid, bias_mid)
    operands = (freq, shift) + weights
    raw_block = pl.pallas_call(
        functools.partial(filter_kernel, length=length),
        grid=(steps,),
        in_specs=[SCALAR] + [const_spec(x) for x in operands + (w_out_t, rates)],
        out_specs=pl.BlockSpec((channels, width // LANES, LANES), lambda i: (0, i, 0)),
        out_shape=shape((channels, block_rows, LANES)),
        scratch_shapes=[vmem((order, feature_rows)), vmem((channels, order))],
        name="filter_rows",
    )(base, *operands, w_out_t, rates)
    raw = lax.all_to_all(
        raw_block.reshape(chan_count, chans, block_rows, LANES),
        "chan", split_axis=0, concat_axis=0, tiled=True,
    )

    chunk = length // chunks
    tables = (first, ahead, back, last, cos_t, sin_t)
    early = lambda i: (0, 0, jnp.minimum(i, chunks - 1))
    late = lambda i: (0, jnp.maximum(i - chunks, 0), 0, 0)
    piece = lambda i: (0, jnp.maximum(i - chunks, 0), 0, 0)
    fm, fg, skip_row, grad_kernel = pl.pallas_call(
        functools.partial(
            spectra_kernel, chunks=chunks, seqs=seqs, chans=chans
        ),
        grid=(chunks + pairs,),
        in_specs=[SCALAR]
        + [pl.BlockSpec((seqs, chans, chunk), early)] * 4
        + [const_spec(x) for x in tables],
        out_specs=[
            pl.BlockSpec((seqs, 1, spec_rows, 2 * LANES), late),
            pl.BlockSpec((seqs, 1, spec_rows, 2 * LANES), late),
            pl.BlockSpec((8, LANES), lambda i: (0, 0)),
        ]
        + [pl.BlockSpec((chan_count, 2, block_rows, LANES), piece)],
        out_shape=[
            shape((seqs, pairs, spec_rows, 2 * LANES), LOW),
            shape((seqs, pairs, spec_rows, 2 * LANES), LOW),
            shape((8, LANES)),
        ]
        + [shape((chan_count, chans, block_rows, LANES))],
        scratch_shapes=[
            vmem((seqs, half * (chans + 1), LANES)),
            vmem((seqs, half * (chans + 1), LANES)),
            vmem((chans, LANES)),
            vmem((2 * seqs, 2 * half, 2 * LANES)),
            vmem((2 * seqs, spec_rows, 2 * LANES), LOW),
            vmem((2 * seqs, spec_rows, 2 * LANES)),
            vmem((spec_rows, 2 * LANES), LOW),
            vmem((spec_rows, 2 * LANES)),
            vmem((2 * half, 2 * LANES), LOW),
        ],
        name="spectra",
    )(base, value, gate_in, gate_out, cotangent, *tables)

    feats, acts, cosines = pl.pallas_call(
        functools.partial(activation_kernel, length=length),
        grid=(steps,),
        in_specs=[SCALAR] + [const_spec(x) for x in operands] + [pl.BlockSpec(memory_space=pl.ANY)],
        out_specs=[
            pl.BlockSpec((feature_rows, width), lambda i: (0, i)),
            pl.BlockSpec((3 * order, width), lambda i: (0, i)),
            pl.BlockSpec((3 * order, width), lambda i: (0, i)),
        ],
        out_shape=[
            shape((feature_rows, block), LOW),
            shape((3 * order, block), LOW),
            shape((3 * order, block), LOW),
        ],
        scratch_shapes=[vmem((order, feature_rows))],
        name="activations",
    )(base, *operands, skip_row)

    together = 2 if pairs % 2 == 0 else 1
    group = 2 * together
    many = 4 if chans % 4 == 0 else 2
    block_spec = lambda n: pl.BlockSpec((chan_count, n, block_rows, LANES), lambda i: (0, i, 0, 0))
    grad_raw, lines = pl.pallas_call(
        functools.partial(norm_kernel, length=length),
        grid=(chans // many,),
        in_specs=[SCALAR, block_spec(many), block_spec(many), pl.BlockSpec(memory_space=pl.ANY)],
        out_specs=[block_spec(many), pl.BlockSpec((8, LANES), lambda i: (0, 0))],
        out_shape=[shape((chan_count, chans, block_rows, LANES)), shape((8, LANES))],
        name="normalization",
    )(base, raw, grad_kernel, feats)
    taken = lax.all_to_all(grad_raw, "chan", split_axis=0, concat_axis=0, tiled=True)
    ahead_tabs = (first, ahead, cos_t, sin_t)
    fk = pl.pallas_call(
        kernel_kernel,
        grid=(pairs // together,),
        in_specs=[block_spec(group), pl.BlockSpec(memory_space=pl.ANY)]
        + [const_spec(x) for x in ahead_tabs],
        out_specs=pl.BlockSpec((together, spec_rows, 2 * LANES), lambda i: (i, 0, 0)),
        out_shape=shape((pairs, spec_rows, 2 * LANES), LOW),
        scratch_shapes=[
            vmem((together, 2 * half, 2 * LANES)),
            vmem((together, spec_rows, 2 * LANES), LOW),
        ],
        name="filter_spectrum",
    )(raw, lines, *ahead_tabs)

    back_tabs = (back, last, cos_t, sin_t)
    skip_line = skip_gain.reshape(1, chans)
    anywhere = pl.BlockSpec(memory_space=pl.ANY)
    together = 4 if pairs % 4 == 0 else together
    out_steps = pairs // together

    out_chunks = 2

    def outputs(b, after, held):
        early4 = lambda i: (b, jnp.minimum(i, out_steps - 1), 0, 0)
        early3 = lambda i: (jnp.minimum(i, out_steps - 1), 0, 0)
        late3 = lambda i: (b, 0, jnp.maximum(i - out_steps, 0))
        signal_spec = pl.BlockSpec((1, chans, length // out_chunks), late3)
        wide_spec = pl.BlockSpec((1, together, spec_rows, 2 * LANES), early4)
        operands = (
            base, fm, fg, fk, value, gate_in, gate_out, cotangent, skip_line, lines,
        ) + back_tabs
        extras = tuple(after) + tuple(held)
        return pl.pallas_call(
            functools.partial(output_kernel, steps=out_steps, chunks=out_chunks, chans=chans),
            grid=(out_steps + out_chunks,),
            in_specs=[SCALAR, wide_spec, wide_spec]
            + [pl.BlockSpec((together, spec_rows, 2 * LANES), early3)]
            + [signal_spec] * 4
            + [const_spec(x) for x in (skip_line, lines) + back_tabs]
            + [anywhere] * len(extras),
            out_specs=[signal_spec] * 3 + [pl.BlockSpec((8, LANES), lambda i: (0, 0))],
            out_shape=[shape((seqs, chans, length), LOW)] * 3 + [shape((8, LANES))],
            input_output_aliases={
                len(operands) + len(after) + n: n for n in range(len(held))
            },
            scratch_shapes=[
                vmem((half * (chans + 1), LANES)),
                vmem((half * (chans + 1), LANES)),
                vmem((together, 2 * spec_rows, 2 * LANES), LOW),
                vmem((together, 2 * spec_rows, 2 * LANES)),
                vmem((together, 2 * half, 4 * LANES), LOW),
            ],
            name="outputs",
        )(*operands, *extras)

    early_count = seqs
    held, token = (), lines
    for b in range(early_count):
        *held, token = outputs(b, (), held)

    packed_rows = -(-(channels + order + 2) // 16) * 16
    wide_spec = lambda rows: pl.BlockSpec((rows, width // LANES, LANES), lambda i: (0, i, 0))
    packed = pl.pallas_call(
        functools.partial(filter_grad_kernel, length=length),
        grid=(steps,),
        in_specs=[
            SCALAR,
            wide_spec(channels),
            pl.BlockSpec((feature_rows, width), lambda i: (0, i)),
            pl.BlockSpec((3 * order, width), lambda i: (0, i)),
            pl.BlockSpec((3 * order, width), lambda i: (0, i)),
        ]
        + [const_spec(x) for x in (weight_mid, w_out_t, rates, lines, skip_row)]
        + [anywhere],
        out_specs=pl.BlockSpec((packed_rows, LANES), lambda i: (0, 0)),
        out_shape=shape((packed_rows, LANES)),
        scratch_shapes=[
            vmem((channels, order)),
            vmem((2, order, order)),
            vmem((order, feature_rows)),
            vmem((3, order, LANES)),
        ],
        name="filter_gradients",
    )(
        base, taken.reshape(channels, block_rows, LANES), feats, acts, cosines, weight_mid,
        w_out_t, rates, lines, skip_row, token,
    )
    for b in range(early_count, seqs):
        *held, token = outputs(b, (packed,), held)
    grad_val, grad_gin, grad_gout = held

    halves = packed.reshape(2, packed_rows // 2, LANES)
    keep = jnp.where(member % 2 == 0, halves[0], halves[1])
    give = jnp.where(member % 2 == 0, halves[1], halves[0])
    own = butterfly(keep + exchange(give, "chan", 1), "chan", 2)
    own = butterfly(own, "seq")
    other = exchange(own, "chan", 1)
    factor = 1.0 / math.sqrt(seqs * seq_count * length)
    d_in_t, d_bin, d_mid, d_bmid, d_out_t, d_rate, d_skip = pl.pallas_call(
        functools.partial(unpack_kernel, scale=factor, features=feature_rows),
        in_specs=[SCALAR, pl.BlockSpec(), pl.BlockSpec()],
        out_shape=[
            shape(weight_in.shape[::-1]),
            shape((1, order)),
            shape(weight_mid.shape),
            shape(bias_mid.shape),
            shape(weight_out.shape[::-1]),
            shape((1, channels)),
            shape((1, chans)),
        ],
        scratch_shapes=[vmem((packed_rows, LANES))],
        name="unpack",
    )(base, own, other)
    return (
        grad_val, grad_gin, grad_gout, d_skip[0],
        d_in_t.T, d_bin[0], d_mid, d_bmid, d_out_t.T, d_rate[0],
    )


def solution(mesh):
    large = P("seq", "chan", None)
    return jax.shard_map(
        local,
        mesh=mesh,
        in_specs=(large,) * 4 + (P("chan"),) + (P(),) * 6,
        out_specs=(large,) * 3 + (P("chan"),) + (P(),) * 6,
        check_vma=False,
    )
```

```python
import functools
import math

import jax
import jax.numpy as jnp
import numpy as np
from jax import lax
from jax.experimental import pallas as pl
from jax.experimental.pallas import tpu as pltpu
from jax.sharding import PartitionSpec as P

EPSILON = 1e-06
LANES = 128
F32 = jnp.float32
LOW = jnp.bfloat16


def band_table(length, bands):
    highest = length / 4.0
    return np.array(
        [math.floor(highest ** (number / (bands - 1)) + 0.5) for number in range(bands)], np.int32
    )


def feature_tables(length, bands, rows):
    freq = np.zeros((rows, LANES), np.int32)
    shift = np.full((rows, LANES), length // 4, np.int32)
    table = band_table(length, bands)[:, None]
    freq[1 : 1 + bands] = table
    shift[1 : 1 + bands] = length // 2
    freq[1 + bands : 1 + 2 * bands] = table
    return freq, shift


def dft_tables(length):
    half = length // LANES
    rows = 2 * half
    k = np.arange(half)[:, None]
    a = np.arange(half)[None, :]
    angle = 2.0 * np.pi / rows * (k * a % rows)
    cos_rows = np.cos(angle)
    sin_rows = np.sin(angle)
    alternating = 1.0 - 2.0 * (np.arange(half) % 2)
    first = np.concatenate([cos_rows, -sin_rows], axis=0)
    first[half] = alternating
    weight = np.full((half, 1), 2.0)
    weight[0] = 1.0
    last = np.concatenate([cos_rows * weight, -sin_rows * weight], axis=0)
    last[half] = alternating
    last = last.T / (2.0 * length)
    col = np.arange(LANES)
    angle = 2.0 * np.pi / LANES * (col[:, None] * col[None, :] % LANES)
    cos_cols, sin_cols = np.cos(angle), np.sin(angle)
    ahead = np.block([[cos_cols, -sin_cols], [sin_cols, cos_cols]])
    back = np.block([[cos_cols, sin_cols], [-sin_cols, cos_cols]])
    total = 2 * length
    twist_rows = np.arange(half + 8)[:, None]
    angle = 2.0 * np.pi / total * (twist_rows * col[None, :] % total)
    low = lambda x: x.astype(np.float32).astype(LOW)
    return (
        low(first),
        low(ahead),
        low(back),
        low(last),
        np.cos(angle).astype(np.float32),
        np.sin(angle).astype(np.float32),
    )


def forward_rows(signal, tabs, r_ref):
    r_ref[...] = jnp.dot(tabs[0][...], signal, preferred_element_type=F32)


def forward_columns(tabs, h_ref):
    return jnp.dot(h_ref[...], tabs[1][...], preferred_element_type=F32)


def forward_pair(signal, tabs, r_ref, h_ref):
    forward_rows(signal, tabs, r_ref)
    forward_twist(tabs, r_ref, h_ref)
    return forward_columns(tabs, h_ref)


def forward_twist(tabs, r_ref, h_ref):
    first, ahead, cos_t, sin_t = tabs
    half = first.shape[1]
    groups = half // 8
    top = lax.broadcasted_iota(jnp.int32, (8, LANES), 0) == 0
    for g in range(groups + 1):
        cosine = cos_t[8 * g : 8 * g + 8, :]
        sine = sin_t[8 * g : 8 * g + 8, :]
        real, imag = [], []
        for c in range(2):
            lanes = slice(LANES * c, LANES * c + LANES)
            if g < groups:
                g_re = r_ref[8 * g : 8 * g + 8, lanes]
                g_im = r_ref[half + 8 * g : half + 8 * g + 8, lanes]
                if g == 0:
                    g_im = jnp.where(top, 0.0, g_im)
                real.append(g_re * cosine + g_im * sine)
                imag.append(g_im * cosine - g_re * sine)
            else:
                g_re = jnp.where(top, r_ref[half : half + 8, lanes], 0.0)
                real.append(g_re * cosine)
                imag.append(-(g_re * sine))
        rows = slice(16 * g, 16 * g + 16)
        h_ref[rows, :LANES] = jnp.concatenate(real, axis=0).astype(LOW)
        h_ref[rows, LANES:] = jnp.concatenate(imag, axis=0).astype(LOW)


def inverse_columns(s_ref, tabs, b_ref):
    b_ref[...] = jnp.dot(s_ref[...], tabs[0][...], preferred_element_type=F32)


def inverse_twist(tabs, b_ref, t_ref):
    _, last, cos_t, sin_t = tabs
    half = last.shape[0]
    groups = half // 8
    top = lax.broadcasted_iota(jnp.int32, (8, LANES), 0) == 0

    def turned(g, c):
        rows = slice(16 * g + 8 * c, 16 * g + 8 * c + 8)
        re, im = b_ref[rows, :LANES], b_ref[rows, LANES:]
        cosine = cos_t[8 * g : 8 * g + 8, :]
        sine = sin_t[8 * g : 8 * g + 8, :]
        return re * cosine - im * sine, re * sine + im * cosine

    for g in range(0, groups, 2):
        for c in range(2):
            lanes = slice(LANES * c, LANES * c + LANES)
            re0, im0 = turned(g, c)
            re1, im1 = turned(g + 1, c)
            if g == 0:
                im0 = jnp.where(top, turned(groups, c)[0], im0)
            t_ref[8 * g : 8 * g + 16, lanes] = jnp.concatenate([re0, re1], axis=0).astype(LOW)
            t_ref[half + 8 * g : half + 8 * g + 16, lanes] = jnp.concatenate(
                [im0, im1], axis=0
            ).astype(LOW)


def inverse_rows(tabs, t_ref):
    return jnp.dot(tabs[1][...], t_ref[...], preferred_element_type=F32)


def inverse_pair(s_ref, tabs, b_ref, t_ref):
    inverse_columns(s_ref, tabs, b_ref)
    inverse_twist(tabs, b_ref, t_ref)
    return inverse_rows(tabs, t_ref)


def staggered(jobs):
    stages = max(len(job) for job in jobs)
    for when in range(len(jobs) + stages - 1):
        for number in reversed(range(len(jobs))):
            stage = when - number
            if 0 <= stage < len(jobs[number]):
                jobs[number][stage]()


def spectra_kernel(
    base_ref, val, gin, gout, cot, first, ahead, back, last, cos_t, sin_t,
    fm_out, fg_out, skip_out, grad_out,
    mix_s, grad_s, skip_s, r_s, h_s, f_s, cross_s, b_s, t_s, *, chunks, seqs, chans,
):
    step = pl.program_id(0)
    chunk_rows = val.shape[2] // LANES
    half = chunk_rows * chunks

    @pl.when(step == 0)
    def _():
        skip_s[...] = jnp.zeros_like(skip_s)

    @pl.when(step < chunks)
    def _():
        for b in range(seqs):
            total = skip_s[...]
            for a in range(chunk_rows):
                lanes = slice(LANES * a, LANES * a + LANES)
                mixed = gin[b, :, lanes].astype(F32) * val[b, :, lanes].astype(F32)
                inner = cot[b, :, lanes].astype(F32) * gout[b, :, lanes].astype(F32)
                rows = pl.ds((step * chunk_rows + a) * (chans + 1), chans)
                mix_s[b, rows, :] = mixed
                grad_s[b, rows, :] = inner
                total = total + mixed * inner
            skip_s[...] = total

    @pl.when(step == chunks - 1)
    def _():
        per_row = jnp.sum(skip_s[...], axis=1, keepdims=True)
        lane = lax.broadcasted_iota(jnp.int32, (chans, LANES), 1)
        row = lax.broadcasted_iota(jnp.int32, (chans, LANES), 0)
        mine = lane == row + base_ref[0]
        spread = jnp.sum(jnp.where(mine, per_row, 0.0), axis=0, keepdims=True)
        top = lax.broadcasted_iota(jnp.int32, (8, LANES), 0) == 0
        skip_out[...] = jnp.where(top, spread, 0.0)

    @pl.when(step >= chunks)
    def _():
        pair = step - chunks
        tabs = (first, ahead, cos_t, sin_t)

        def job(number):
            b, inner = number // 2, number % 2 == 1
            source, target = (grad_s, fg_out) if inner else (mix_s, fm_out)
            r_ref, h_ref = r_s.at[number], h_s.at[number]

            def rows():
                parts = [
                    source[b, pl.ds(2 * pair + c, half, stride=chans + 1), :] for c in range(2)
                ]
                forward_rows(jnp.concatenate(parts, axis=1).astype(LOW), tabs, r_ref)

            def twist():
                forward_twist(tabs, r_ref, h_ref)

            def columns():
                f_s[number] = forward_columns(tabs, h_ref)
                target[b, 0] = f_s[number].astype(LOW)

            return rows, twist, columns

        staggered([job(number) for number in range(2 * seqs)])
        for g in range(half // 8 + 1):
            rows = slice(16 * g, 16 * g + 16)
            cross_re = cross_im = None
            for b in range(seqs):
                m_re, m_im = f_s[2 * b, rows, :LANES], f_s[2 * b, rows, LANES:]
                g_re, g_im = f_s[2 * b + 1, rows, :LANES], f_s[2 * b + 1, rows, LANES:]
                c_re = m_re * g_re + m_im * g_im
                c_im = m_re * g_im - m_im * g_re
                cross_re = c_re if b == 0 else cross_re + c_re
                cross_im = c_im if b == 0 else cross_im + c_im
            cross_s[rows, :LANES] = cross_re.astype(LOW)
            cross_s[rows, LANES:] = cross_im.astype(LOW)
        y = inverse_pair(cross_s, (back, last, cos_t, sin_t), b_s, t_s)
        members, _, each, _ = grad_out.shape
        for c in range(2):
            lanes = slice(LANES * c, LANES * c + LANES)
            grad_out[:, c] = y[:, lanes].reshape(members, each, LANES)


def norm_kernel(base_ref, raw, grads, after, grad_out, lines_out, *, length):
    step = pl.program_id(0)
    blocks, channels, rows_each, _ = raw.shape
    half = blocks * rows_each
    lane = lax.broadcasted_iota(jnp.int32, (8, LANES), 1)
    line = lax.broadcasted_iota(jnp.int32, (8, LANES), 0)
    position = (
        lax.broadcasted_iota(jnp.int32, (half, LANES), 0) * LANES
        + lax.broadcasted_iota(jnp.int32, (half, LANES), 1)
    ).astype(F32) * (-1.0 / length)

    @pl.when(step == 0)
    def _():
        lines_out[...] = jnp.zeros_like(lines_out)

    total = lines_out[...]
    for c in range(channels):
        row, grad = raw[:, c].reshape(half, LANES), grads[:, c].reshape(half, LANES)
        square_rows, cross_rows = row * row, row * grad
        square = jnp.sum(square_rows, keepdims=True) + EPSILON
        inv = 1.0 / jnp.sqrt(square)
        coef = jnp.sum(cross_rows, keepdims=True) * (inv / square)
        rate = inv * jnp.sum(cross_rows * position, keepdims=True) - coef * jnp.sum(
            square_rows * position, keepdims=True
        )
        grad_out[:, c] = (grad * inv - row * coef).reshape(blocks, rows_each, LANES)
        mine = lane == base_ref[0] + channels * step + c
        for number, x in enumerate((inv, rate)):
            total = jnp.where(jnp.logical_and(mine, line == number), x, total)
    lines_out[...] = total


def kernel_kernel(raw, after, first, ahead, cos_t, sin_t, fk_out, r_s, h_s):
    blocks, channels, rows_each, _ = raw.shape
    half = blocks * rows_each
    tabs = (first, ahead, cos_t, sin_t)

    def job(number):
        def rows():
            parts = [raw[:, 2 * number + c].reshape(half, LANES) for c in range(2)]
            signal = jnp.concatenate(parts, axis=1).astype(LOW)
            forward_rows(signal, tabs, r_s.at[number])

        def twist():
            forward_twist(tabs, r_s.at[number], h_s.at[number])

        def columns():
            fk_out[number] = forward_columns(tabs, h_s.at[number]).astype(LOW)

        return rows, twist, columns

    staggered([job(number) for number in range(channels // 2)])


def output_kernel(
    base_ref, fm, fg, fk, val, gin, gout, cot, skip, lines, back, last, cos_t, sin_t, *rest,
    steps, chunks, chans,
):
    val_out, gin_out, gout_out, token, conv_s, corr_s, s_s, b_s, t_s = rest[-9:]
    step = pl.program_id(0)
    chunk_rows = val.shape[2] // LANES
    half = chunk_rows * chunks
    together = fk.shape[0]

    @pl.when(step < steps)
    def _():
        tabs = (back, last, cos_t, sin_t)

        height = 2 * (half + 8)

        def job(p):
            s_ref, b_ref, t_ref = s_s.at[p], b_s.at[p], t_s.at[p]

            def product():
                for g in range(half // 8 + 1):
                    rows = slice(16 * g, 16 * g + 16)
                    lower = slice(height + 16 * g, height + 16 * g + 16)
                    k_re, k_im = fk[p, rows, :LANES].astype(F32), fk[p, rows, LANES:].astype(F32)
                    re, im = fm[0, p, rows, :LANES].astype(F32), fm[0, p, rows, LANES:].astype(F32)
                    s_ref[rows, :LANES] = (re * k_re - im * k_im).astype(LOW)
                    s_ref[rows, LANES:] = (re * k_im + im * k_re).astype(LOW)
                    re, im = fg[0, p, rows, :LANES].astype(F32), fg[0, p, rows, LANES:].astype(F32)
                    s_ref[lower, :LANES] = (re * k_re + im * k_im).astype(LOW)
                    s_ref[lower, LANES:] = (im * k_re - re * k_im).astype(LOW)

            def columns():
                inverse_columns(s_ref, tabs, b_ref)

            def twist():
                for number in range(2):
                    inverse_twist(
                        tabs,
                        b_ref.at[height * number : height * number + height],
                        t_ref.at[:, 2 * LANES * number : 2 * LANES * number + 2 * LANES],
                    )

            def finish():
                y = inverse_rows(tabs, t_ref)
                for number, target in enumerate((conv_s, corr_s)):
                    for c in range(2):
                        channel = 2 * (step * together + p) + c
                        lanes = LANES * (2 * number + c)
                        target[pl.ds(channel, half, stride=chans + 1), :] = y[
                            :, lanes : lanes + LANES
                        ]

            return product, columns, twist, finish

        staggered([job(p) for p in range(together)])

    @pl.when(step >= steps)
    def _():
        chunk = step - steps
        token[...] = jnp.zeros_like(token)
        gain = jnp.broadcast_to(column(skip[...], chans), (chans, LANES))
        lane = lax.broadcasted_iota(jnp.int32, (chans, LANES), 1)
        row = lax.broadcasted_iota(jnp.int32, (chans, LANES), 0)
        inv = jnp.sum(
            jnp.where(lane == row + base_ref[0], lines[0:1, :], 0.0), axis=1, keepdims=True
        )
        inv = jnp.broadcast_to(inv, (chans, LANES))
        for a in range(chunk_rows):
            lanes = slice(LANES * a, LANES * a + LANES)
            rows = pl.ds((chunk * chunk_rows + a) * (chans + 1), chans)
            v = val[0, :, lanes].astype(F32)
            gi = gin[0, :, lanes].astype(F32)
            go = gout[0, :, lanes].astype(F32)
            co = cot[0, :, lanes].astype(F32)
            inner = inv * conv_s[rows, :] + gain * (gi * v)
            grad_mixed = inv * corr_s[rows, :] + gain * (co * go)
            gout_out[0, :, lanes] = (co * inner).astype(LOW)
            val_out[0, :, lanes] = (grad_mixed * gi).astype(LOW)
            gin_out[0, :, lanes] = (grad_mixed * v).astype(LOW)


INV_PI = 0.3183098861837907
PI_HIGH = 3.140625
PI_LOW = 9.676535897932795e-4


def fit(function, powers, top):
    nodes = np.cos(np.pi * (np.arange(400) + 0.5) / 800) * top
    design = np.stack([nodes**p for p in powers], axis=1)
    return [float(x) for x in np.linalg.lstsq(design, function(nodes), rcond=None)[0]]


SINE = fit(lambda x: np.sin(x) - x, (3, 5, 7, 9), np.pi / 2 + 1e-3)
COSINE = fit(lambda x: np.cos(x) - 1.0, (2, 4, 6, 8), np.pi / 2 + 1e-3)


def poly(coefficients, r2):
    p = coefficients[-1]
    for c in coefficients[-2::-1]:
        p = c + r2 * p
    return r2 * p


def sine_poly(r, r2):
    return r + r * poly(SINE, r2)


def cosine_poly(r2):
    return 1.0 + poly(COSINE, r2)


def sine_cosine(z):
    turns = jnp.floor(z * INV_PI + 0.5)
    r = (z - turns * PI_HIGH) - turns * PI_LOW
    halves = turns * 0.5
    sign = 1.0 - 4.0 * (halves - jnp.floor(halves))
    r2 = r * r
    return sign * sine_poly(r, r2), sign * cosine_poly(r2)


def column(row, size):
    lane = lax.broadcasted_iota(jnp.int32, (size, size), 1)
    diagonal = lane == lax.broadcasted_iota(jnp.int32, (size, size), 0)
    return jnp.sum(jnp.where(diagonal, row, 0.0), axis=1, keepdims=True)


def split(x):
    high = x.astype(LOW)
    return high, (x - high.astype(F32)).astype(LOW)


def triple_dot(weight, x):
    w_high, w_low = split(weight)
    x_high, x_low = split(x)
    wide = jnp.concatenate([w_high, w_high, w_low], axis=1)
    tall = jnp.concatenate([x_high, x_low, x_high], axis=0)
    return jnp.dot(wide, tall, preferred_element_type=F32)


def decay_tables(rates, start, channels, length):
    rate = column(rates, channels) * (-1.0 / length)
    lane = lax.broadcasted_iota(jnp.int32, (channels, LANES), 1)
    fine = jnp.exp(rate * lane.astype(F32))
    coarse = jnp.exp(rate * (start + LANES * lane).astype(F32))
    return fine, coarse


def sine(z):
    turns = jnp.floor(z * INV_PI + 0.5)
    r = (z - turns * PI_HIGH) - turns * PI_LOW
    halves = turns * 0.5
    sign = 1.0 - 4.0 * (halves - jnp.floor(halves))
    return sign * sine_poly(r, r * r)


def features(start, freq, shift, width, length):
    rows = freq.shape[0]
    position = start + lax.broadcasted_iota(jnp.int32, (rows, width), 1)
    freq_w = jnp.concatenate([freq[...]] * (width // LANES), axis=1)
    shift_w = jnp.concatenate([shift[...]] * (width // LANES), axis=1)
    quarter = length // 4
    phase = position * freq_w + shift_w
    sign = (1 - ((phase >> int(math.log2(length // 2))) & 1) * 2).astype(F32)
    angle = ((phase & (length // 2 - 1)) - quarter).astype(F32) * (2.0 * math.pi / length)
    wave = sign * sine_poly(angle, angle * angle)
    linear = lax.broadcasted_iota(jnp.int32, (rows, width), 0) == 0
    return jnp.where(linear, position.astype(F32) * (1.0 / length), wave)


def widen(w_in, w_in_t):
    w_in[...] = jnp.zeros_like(w_in)
    w_in[:, : w_in_t.shape[0]] = w_in_t[...].T


def filter_kernel(
    start_ref, freq, shift, w_in_t, b_in, w_mid, b_mid, w_out_t, rates,
    raw_out, w_in, w_out, *, length,
):
    width = raw_out.shape[1] * LANES
    order = w_mid.shape[1]
    channels = w_out_t.shape[1]

    @pl.when(pl.program_id(0) == 0)
    def _():
        widen(w_in, w_in_t)
        w_out[...] = w_out_t[...].T

    start = start_ref[3] + pl.program_id(0) * width
    hidden = features(start, freq, shift, width, length)
    weights = ((w_in[...], b_in[...]), (w_mid[0], b_mid[0:1, :]), (w_mid[1], b_mid[1:2, :]))
    for weight, bias in weights:
        hidden = sine(triple_dot(weight, hidden) + column(bias, order))
    shaped = triple_dot(w_out[...], hidden)
    fine, coarse = decay_tables(rates[...], start, channels, length)
    for a in range(width // LANES):
        decay = fine * coarse[:, a : a + 1]
        raw_out[:, a, :] = shaped[:, LANES * a : LANES * a + LANES] * decay


def activation_kernel(
    start_ref, freq, shift, w_in_t, b_in, w_mid, b_mid, after,
    feat_out, act_out, cos_out, w_in, *, length,
):
    width = feat_out.shape[1]
    order = w_mid.shape[1]

    @pl.when(pl.program_id(0) == 0)
    def _():
        widen(w_in, w_in_t)

    start = start_ref[3] + pl.program_id(0) * width
    hidden = features(start, freq, shift, width, length)
    feat_out[...] = hidden.astype(LOW)
    weights = ((w_in[...], b_in[...]), (w_mid[0], b_mid[0:1, :]), (w_mid[1], b_mid[1:2, :]))
    for number, (weight, bias) in enumerate(weights):
        z = triple_dot(weight, hidden) + column(bias, order)
        hidden, cosine = sine_cosine(z)
        rows = slice(order * number, order * number + order)
        act_out[rows, :] = hidden.astype(LOW)
        cos_out[rows, :] = cosine.astype(LOW)


def double_dot(weight, x):
    wide = jnp.concatenate(split(weight), axis=1)
    return jnp.dot(wide, jnp.concatenate([x, x], axis=0), preferred_element_type=F32)


def nt_dot(x, y):
    return lax.dot_general(x, y, (((1,), (1,)), ((), ())), preferred_element_type=F32)


def filter_grad_kernel(
    start_ref, grad, feat, act, cosines, w_mid, w_out_t, rates, lines, skip_row, token,
    keep, give, d_out, d_mid, d_in, d_bias, packed, *, length,
):
    step = pl.program_id(0)
    width = feat.shape[1]
    order = w_mid.shape[1]
    channels = w_out_t.shape[1]
    start = start_ref[3] + step * width

    @pl.when(step == 0)
    def _():
        for ref in (d_out, d_mid, d_in, d_bias):
            ref[...] = jnp.zeros_like(ref)

    fine, coarse = decay_tables(rates[...], start, channels, length)
    parts = [grad[:, a, :] * (fine * coarse[:, a : a + 1]) for a in range(width // LANES)]
    d_shaped = jnp.concatenate(parts, axis=1)

    def part(ref, number):
        return ref[order * number : order * number + order, :]

    def bias_sum(x, number):
        total = x[:, :LANES]
        for a in range(1, width // LANES):
            total = total + x[:, LANES * a : LANES * a + LANES]
        d_bias[number] = d_bias[number] + total

    low = d_shaped.astype(LOW)
    d_out[...] = d_out[...] + nt_dot(low, part(act, 2))
    dz = double_dot(w_out_t[...], low) * part(cosines, 2).astype(F32)
    bias_sum(dz, 2)
    low = dz.astype(LOW)
    d_mid[1] = d_mid[1] + nt_dot(low, part(act, 1))
    dz = double_dot(w_mid[1].T, low) * part(cosines, 1).astype(F32)
    bias_sum(dz, 1)
    low = dz.astype(LOW)
    d_mid[0] = d_mid[0] + nt_dot(low, part(act, 0))
    dz = double_dot(w_mid[0].T, low) * part(cosines, 0).astype(F32)
    bias_sum(dz, 0)
    d_in[...] = d_in[...] + nt_dot(dz.astype(LOW), feat[...])

    @pl.when(step == pl.num_programs(0) - 1)
    def _():
        packed[...] = jnp.zeros_like(packed)
        packed[:channels, :order] = d_out[...]
        packed[:order, order : 2 * order] = d_mid[0]
        packed[order : 2 * order, order : 2 * order] = d_mid[1]
        base = channels
        features = d_in.shape[1]
        packed[base : base + order, :features] = d_in[...]
        spot = lax.broadcasted_iota(jnp.int32, (order, LANES), 1)
        current = packed[base : base + order, :]
        for number in range(3):
            total = jnp.sum(d_bias[number], axis=1, keepdims=True)
            current = jnp.where(spot == features + number, total, current)
        packed[base : base + order, :] = current
        base += order
        packed[base : base + 1, :] = lines[1:2, :]
        packed[base + 1 : base + 2, :] = skip_row[0:1, :]
        size = keep.shape[0]
        bit = start_ref[2]
        keep[...] = packed[pl.ds(pl.multiple_of(bit * size, 8), size), :]
        give[...] = packed[pl.ds(pl.multiple_of((1 - bit) * size, 8), size), :]


def unpack_kernel(
    base_ref, own, other, w_in_t, b_in, w_mid, b_mid, w_out_t, rate, skip, whole,
    *, scale, features,
):
    size = own.shape[0]
    bit = base_ref[2]
    whole[pl.ds(pl.multiple_of(bit * size, 8), size), :] = own[...] * scale
    whole[pl.ds(pl.multiple_of((1 - bit) * size, 8), size), :] = other[...] * scale
    order, channels = w_out_t.shape
    w_out_t[...] = whole[:channels, :].T[:order, :]
    mid = whole[: 2 * order, order : 2 * order]
    w_mid[0] = mid[:order]
    w_mid[1] = mid[order:]
    base = channels
    block = whole[base : base + order, :]
    w_in_t[...] = block.T[: w_in_t.shape[0], :]
    lane = lax.broadcasted_iota(jnp.int32, (order, LANES), 1)
    row = lax.broadcasted_iota(jnp.int32, (order, LANES), 0)

    def as_row(number):
        values = jnp.sum(jnp.where(lane == features + number, block, 0.0), axis=1, keepdims=True)
        return jnp.sum(jnp.where(lane == row, values, 0.0), axis=0, keepdims=True)[:, :order]

    b_in[...] = as_row(0)
    b_mid[0:1, :] = as_row(1)
    b_mid[1:2, :] = as_row(2)
    base += order
    rate[...] = whole[base : base + 1, :channels]
    chans = skip.shape[1]
    skips = whole[base + 1 : base + 2, :]
    lane = lax.broadcasted_iota(jnp.int32, (chans, LANES), 1)
    row = lax.broadcasted_iota(jnp.int32, (chans, LANES), 0)
    values = jnp.sum(jnp.where(lane == row + base_ref[0], skips, 0.0), axis=1, keepdims=True)
    skip[...] = jnp.sum(jnp.where(lane == row, values, 0.0), axis=0, keepdims=True)[:, :chans]


def const_spec(array):
    zeros = (0,) * len(array.shape)
    return pl.BlockSpec(array.shape, lambda i: zeros)


SCALAR = pl.BlockSpec(memory_space=pltpu.SMEM)


def vmem(shape, dtype=F32):
    return pltpu.VMEM(shape, dtype)


def shape(dims, dtype=F32):
    return jax.ShapeDtypeStruct(dims, dtype)


def exchange(x, axis, bit):
    size = lax.axis_size(axis)
    return lax.ppermute(x, axis, [(s, s ^ bit) for s in range(size)])


def fan_sum(x, axis, step):
    others = [exchange(x, axis, bit) for bit in range(step, lax.axis_size(axis), step)]
    return functools.reduce(jnp.add, others, x)


def local(
    value, gate_in, gate_out, cotangent, skip_gain,
    weight_in, bias_in, weight_mid, bias_mid, weight_out, decay_rate,
):
    seqs, chans, length = value.shape
    channels, order = weight_out.shape
    chan_count = lax.axis_size("chan")
    seq_count = lax.axis_size("seq")
    block = length // chan_count
    block_rows = block // LANES
    half = length // LANES
    pairs = chans // 2
    spec_rows = 2 * (half + 8)
    chunks = 4
    member = lax.axis_index("chan").astype(jnp.int32)
    base = jnp.stack([member * chans, member, member % 2, member * block])
    first, ahead, back, last, cos_t, sin_t = [jnp.asarray(t) for t in dft_tables(length)]
    feature_rows = 48
    bands = (weight_in.shape[1] - 1) // 2
    freq, shift = [jnp.asarray(t) for t in feature_tables(length, bands, feature_rows)]

    width = min(2048, block)
    steps = block // width
    rates = decay_rate.reshape(1, channels)
    w_out_t = weight_out.T
    w_in_t = weight_in.T
    weights = (w_in_t, bias_in.reshape(1, order), weight_mid, bias_mid)
    operands = (freq, shift) + weights
    raw_block = pl.pallas_call(
        functools.partial(filter_kernel, length=length),
        grid=(steps,),
        in_specs=[SCALAR] + [const_spec(x) for x in operands + (w_out_t, rates)],
        out_specs=pl.BlockSpec((channels, width // LANES, LANES), lambda i: (0, i, 0)),
        out_shape=shape((channels, block_rows, LANES)),
        scratch_shapes=[vmem((order, feature_rows)), vmem((channels, order))],
        name="filter_rows",
    )(base, *operands, w_out_t, rates)
    raw = lax.all_to_all(
        raw_block.reshape(chan_count, chans, block_rows, LANES),
        "chan", split_axis=0, concat_axis=0, tiled=True,
    )

    chunk = length // chunks
    tables = (first, ahead, back, last, cos_t, sin_t)
    early = lambda i: (0, 0, jnp.minimum(i, chunks - 1))
    late = lambda i: (0, jnp.maximum(i - chunks, 0), 0, 0)
    piece = lambda i: (0, jnp.maximum(i - chunks, 0), 0, 0)
    fm, fg, skip_row, grad_kernel = pl.pallas_call(
        functools.partial(
            spectra_kernel, chunks=chunks, seqs=seqs, chans=chans
        ),
        grid=(chunks + pairs,),
        in_specs=[SCALAR]
        + [pl.BlockSpec((seqs, chans, chunk), early)] * 4
        + [const_spec(x) for x in tables],
        out_specs=[
            pl.BlockSpec((seqs, 1, spec_rows, 2 * LANES), late),
            pl.BlockSpec((seqs, 1, spec_rows, 2 * LANES), late),
            pl.BlockSpec((8, LANES), lambda i: (0, 0)),
        ]
        + [pl.BlockSpec((chan_count, 2, block_rows, LANES), piece)],
        out_shape=[
            shape((seqs, pairs, spec_rows, 2 * LANES), LOW),
            shape((seqs, pairs, spec_rows, 2 * LANES), LOW),
            shape((8, LANES)),
        ]
        + [shape((chan_count, chans, block_rows, LANES))],
        scratch_shapes=[
            vmem((seqs, half * (chans + 1) + 16, LANES)),
            vmem((seqs, half * (chans + 1) + 16, LANES)),
            vmem((chans, LANES)),
            vmem((2 * seqs, 2 * half, 2 * LANES)),
            vmem((2 * seqs, spec_rows, 2 * LANES), LOW),
            vmem((2 * seqs, spec_rows, 2 * LANES)),
            vmem((spec_rows, 2 * LANES), LOW),
            vmem((spec_rows, 2 * LANES)),
            vmem((2 * half, 2 * LANES), LOW),
        ],
        name="spectra",
    )(base, value, gate_in, gate_out, cotangent, *tables)

    feats, acts, cosines = pl.pallas_call(
        functools.partial(activation_kernel, length=length),
        grid=(steps,),
        in_specs=[SCALAR] + [const_spec(x) for x in operands] + [pl.BlockSpec(memory_space=pl.ANY)],
        out_specs=[
            pl.BlockSpec((feature_rows, width), lambda i: (0, i)),
            pl.BlockSpec((3 * order, width), lambda i: (0, i)),
            pl.BlockSpec((3 * order, width), lambda i: (0, i)),
        ],
        out_shape=[
            shape((feature_rows, block), LOW),
            shape((3 * order, block), LOW),
            shape((3 * order, block), LOW),
        ],
        scratch_shapes=[vmem((order, feature_rows))],
        name="activations",
    )(base, *operands, skip_row)

    together = 4 if pairs % 4 == 0 else 1
    group = 2 * together
    many = 8 if chans % 8 == 0 else 2
    block_spec = lambda n: pl.BlockSpec((chan_count, n, block_rows, LANES), lambda i: (0, i, 0, 0))
    grad_raw, lines = pl.pallas_call(
        functools.partial(norm_kernel, length=length),
        grid=(chans // many,),
        in_specs=[SCALAR, block_spec(many), block_spec(many), pl.BlockSpec(memory_space=pl.ANY)],
        out_specs=[block_spec(many), pl.BlockSpec((8, LANES), lambda i: (0, 0))],
        out_shape=[shape((chan_count, chans, block_rows, LANES)), shape((8, LANES))],
        name="normalization",
    )(base, raw, grad_kernel, feats)
    taken = lax.all_to_all(grad_raw, "chan", split_axis=0, concat_axis=0, tiled=True)
    ahead_tabs = (first, ahead, cos_t, sin_t)
    fk = pl.pallas_call(
        kernel_kernel,
        grid=(pairs // together,),
        in_specs=[block_spec(group), pl.BlockSpec(memory_space=pl.ANY)]
        + [const_spec(x) for x in ahead_tabs],
        out_specs=pl.BlockSpec((together, spec_rows, 2 * LANES), lambda i: (i, 0, 0)),
        out_shape=shape((pairs, spec_rows, 2 * LANES), LOW),
        scratch_shapes=[
            vmem((together, 2 * half, 2 * LANES)),
            vmem((together, spec_rows, 2 * LANES), LOW),
        ],
        name="filter_spectrum",
    )(raw, lines, *ahead_tabs)

    back_tabs = (back, last, cos_t, sin_t)
    skip_line = skip_gain.reshape(1, chans)
    anywhere = pl.BlockSpec(memory_space=pl.ANY)
    out_steps = pairs // together

    out_chunks = 2

    def outputs(b, after, held):
        early4 = lambda i: (b, jnp.minimum(i, out_steps - 1), 0, 0)
        early3 = lambda i: (jnp.minimum(i, out_steps - 1), 0, 0)
        late3 = lambda i: (b, 0, jnp.maximum(i - out_steps, 0))
        signal_spec = pl.BlockSpec((1, chans, length // out_chunks), late3)
        wide_spec = pl.BlockSpec((1, together, spec_rows, 2 * LANES), early4)
        operands = (
            base, fm, fg, fk, value, gate_in, gate_out, cotangent, skip_line, lines,
        ) + back_tabs
        extras = tuple(after) + tuple(held)
        return pl.pallas_call(
            functools.partial(output_kernel, steps=out_steps, chunks=out_chunks, chans=chans),
            grid=(out_steps + out_chunks,),
            in_specs=[SCALAR, wide_spec, wide_spec]
            + [pl.BlockSpec((together, spec_rows, 2 * LANES), early3)]
            + [signal_spec] * 4
            + [const_spec(x) for x in (skip_line, lines) + back_tabs]
            + [anywhere] * len(extras),
            out_specs=[signal_spec] * 3 + [pl.BlockSpec((8, LANES), lambda i: (0, 0))],
            out_shape=[shape((seqs, chans, length), LOW)] * 3 + [shape((8, LANES))],
            input_output_aliases={
                len(operands) + len(after) + n: n for n in range(len(held))
            },
            scratch_shapes=[
                vmem((half * (chans + 1) + 16, LANES)),
                vmem((half * (chans + 1) + 16, LANES)),
                vmem((together, 2 * spec_rows, 2 * LANES), LOW),
                vmem((together, 2 * spec_rows, 2 * LANES)),
                vmem((together, 2 * half, 4 * LANES), LOW),
            ],
            name="outputs",
        )(*operands, *extras)

    held, token = (), lines
    for b in range(seqs):
        *held, token = outputs(b, (), held)

    packed_rows = -(-(channels + order + 2) // 16) * 16
    wide_spec = lambda rows: pl.BlockSpec((rows, width // LANES, LANES), lambda i: (0, i, 0))
    keep, give = pl.pallas_call(
        functools.partial(filter_grad_kernel, length=length),
        grid=(steps,),
        in_specs=[
            SCALAR,
            wide_spec(channels),
            pl.BlockSpec((feature_rows, width), lambda i: (0, i)),
            pl.BlockSpec((3 * order, width), lambda i: (0, i)),
            pl.BlockSpec((3 * order, width), lambda i: (0, i)),
        ]
        + [const_spec(x) for x in (weight_mid, w_out_t, rates, lines, skip_row)]
        + [anywhere],
        out_specs=[pl.BlockSpec((packed_rows // 2, LANES), lambda i: (0, 0))] * 2,
        out_shape=[shape((packed_rows // 2, LANES))] * 2,
        scratch_shapes=[
            vmem((channels, order)),
            vmem((2, order, order)),
            vmem((order, feature_rows)),
            vmem((3, order, LANES)),
            vmem((packed_rows, LANES)),
        ],
        name="filter_gradients",
    )(
        base, taken.reshape(channels, block_rows, LANES), feats, acts, cosines, weight_mid,
        w_out_t, rates, lines, skip_row, token,
    )
    grad_val, grad_gin, grad_gout = held

    own = fan_sum(keep + exchange(give, "chan", 1), "chan", 2)
    own = fan_sum(own, "seq", 1)
    other = exchange(own, "chan", 1)
    factor = 1.0 / math.sqrt(seqs * seq_count * length)
    d_in_t, d_bin, d_mid, d_bmid, d_out_t, d_rate, d_skip = pl.pallas_call(
        functools.partial(unpack_kernel, scale=factor, features=feature_rows),
        in_specs=[SCALAR, pl.BlockSpec(), pl.BlockSpec()],
        out_shape=[
            shape(weight_in.shape[::-1]),
            shape((1, order)),
            shape(weight_mid.shape),
            shape(bias_mid.shape),
            shape(weight_out.shape[::-1]),
            shape((1, channels)),
            shape((1, chans)),
        ],
        scratch_shapes=[vmem((packed_rows, LANES))],
        name="unpack",
    )(base, own, other)
    return (
        grad_val, grad_gin, grad_gout, d_skip[0],
        d_in_t.T, d_bin[0], d_mid, d_bmid, d_out_t.T, d_rate[0],
    )


def solution(mesh):
    large = P("seq", "chan", None)
    return jax.shard_map(
        local,
        mesh=mesh,
        in_specs=(large,) * 4 + (P("chan"),) + (P(),) * 6,
        out_specs=(large,) * 3 + (P("chan"),) + (P(),) * 6,
        check_vma=False,
    )
```

```python
import functools
import math

import jax
import jax.numpy as jnp
import numpy as np
from jax import lax
from jax.experimental import pallas as pl
from jax.experimental.pallas import tpu as pltpu
from jax.sharding import PartitionSpec as P

EPSILON = 1e-06
LANES = 128
F32 = jnp.float32
LOW = jnp.bfloat16


def band_table(length, bands):
    highest = length / 4.0
    return np.array(
        [math.floor(highest ** (number / (bands - 1)) + 0.5) for number in range(bands)], np.int32
    )


def feature_tables(length, bands, rows):
    freq = np.zeros((rows, LANES), np.int32)
    shift = np.full((rows, LANES), length // 4, np.int32)
    table = band_table(length, bands)[:, None]
    freq[1 : 1 + bands] = table
    shift[1 : 1 + bands] = length // 2
    freq[1 + bands : 1 + 2 * bands] = table
    return freq, shift


def dft_tables(length):
    half = length // LANES
    rows = 2 * half
    k = np.arange(half)[:, None]
    a = np.arange(half)[None, :]
    angle = 2.0 * np.pi / rows * (k * a % rows)
    cos_rows = np.cos(angle)
    sin_rows = np.sin(angle)
    alternating = 1.0 - 2.0 * (np.arange(half) % 2)
    first = np.concatenate([cos_rows, -sin_rows], axis=0)
    first[half] = alternating
    weight = np.full((half, 1), 2.0)
    weight[0] = 1.0
    last = np.concatenate([cos_rows * weight, -sin_rows * weight], axis=0)
    last[half] = alternating
    last = last.T / (2.0 * length)
    col = np.arange(LANES)
    angle = 2.0 * np.pi / LANES * (col[:, None] * col[None, :] % LANES)
    cos_cols, sin_cols = np.cos(angle), np.sin(angle)
    ahead = np.block([[cos_cols, -sin_cols], [sin_cols, cos_cols]])
    back = np.block([[cos_cols, sin_cols], [-sin_cols, cos_cols]])
    total = 2 * length
    twist_rows = np.arange(half + 8)[:, None]
    angle = 2.0 * np.pi / total * (twist_rows * col[None, :] % total)
    low = lambda x: x.astype(np.float32).astype(LOW)
    return (
        low(first),
        low(ahead),
        low(back),
        low(last),
        np.cos(angle).astype(np.float32),
        np.sin(angle).astype(np.float32),
    )


def forward_rows(signal, tabs, r_ref):
    r_ref[...] = jnp.dot(tabs[0][...], signal, preferred_element_type=F32)


def forward_columns(tabs, h_ref):
    return jnp.dot(h_ref[...], tabs[1][...], preferred_element_type=F32)


def forward_pair(signal, tabs, r_ref, h_ref):
    forward_rows(signal, tabs, r_ref)
    forward_twist(tabs, r_ref, h_ref)
    return forward_columns(tabs, h_ref)


def forward_twist(tabs, r_ref, h_ref):
    first, ahead, cos_t, sin_t = tabs
    half = first.shape[1]
    groups = half // 8
    top = lax.broadcasted_iota(jnp.int32, (8, LANES), 0) == 0
    for g in range(groups + 1):
        cosine = cos_t[8 * g : 8 * g + 8, :]
        sine = sin_t[8 * g : 8 * g + 8, :]
        real, imag = [], []
        for c in range(2):
            lanes = slice(LANES * c, LANES * c + LANES)
            if g < groups:
                g_re = r_ref[8 * g : 8 * g + 8, lanes]
                g_im = r_ref[half + 8 * g : half + 8 * g + 8, lanes]
                if g == 0:
                    g_im = jnp.where(top, 0.0, g_im)
                real.append(g_re * cosine + g_im * sine)
                imag.append(g_im * cosine - g_re * sine)
            else:
                g_re = jnp.where(top, r_ref[half : half + 8, lanes], 0.0)
                real.append(g_re * cosine)
                imag.append(-(g_re * sine))
        rows = slice(16 * g, 16 * g + 16)
        h_ref[rows, :LANES] = jnp.concatenate(real, axis=0).astype(LOW)
        h_ref[rows, LANES:] = jnp.concatenate(imag, axis=0).astype(LOW)


def inverse_columns(s_ref, tabs, b_ref):
    b_ref[...] = jnp.dot(s_ref[...], tabs[0][...], preferred_element_type=F32)


def inverse_twist(tabs, b_ref, t_ref):
    _, last, cos_t, sin_t = tabs
    half = last.shape[0]
    groups = half // 8
    top = lax.broadcasted_iota(jnp.int32, (8, LANES), 0) == 0

    def turned(g, c):
        rows = slice(16 * g + 8 * c, 16 * g + 8 * c + 8)
        re, im = b_ref[rows, :LANES], b_ref[rows, LANES:]
        cosine = cos_t[8 * g : 8 * g + 8, :]
        sine = sin_t[8 * g : 8 * g + 8, :]
        return re * cosine - im * sine, re * sine + im * cosine

    for g in range(0, groups, 2):
        for c in range(2):
            lanes = slice(LANES * c, LANES * c + LANES)
            re0, im0 = turned(g, c)
            re1, im1 = turned(g + 1, c)
            if g == 0:
                im0 = jnp.where(top, turned(groups, c)[0], im0)
            t_ref[8 * g : 8 * g + 16, lanes] = jnp.concatenate([re0, re1], axis=0).astype(LOW)
            t_ref[half + 8 * g : half + 8 * g + 16, lanes] = jnp.concatenate(
                [im0, im1], axis=0
            ).astype(LOW)


def inverse_rows(tabs, t_ref):
    return jnp.dot(tabs[1][...], t_ref[...], preferred_element_type=F32)


def inverse_pair(s_ref, tabs, b_ref, t_ref):
    inverse_columns(s_ref, tabs, b_ref)
    inverse_twist(tabs, b_ref, t_ref)
    return inverse_rows(tabs, t_ref)


def staggered(jobs):
    stages = max(len(job) for job in jobs)
    for when in range(len(jobs) + stages - 1):
        for number in reversed(range(len(jobs))):
            stage = when - number
            if 0 <= stage < len(jobs[number]):
                jobs[number][stage]()


def spectra_kernel(
    base_ref, val, gin, gout, cot, first, ahead, back, last, cos_t, sin_t,
    fm_out, fg_out, skip_out, grad_out,
    mix_s, grad_s, skip_s, r_s, h_s, f_s, cross_s, b_s, t_s, *, chunks, seqs, chans,
):
    step = pl.program_id(0)
    chunk_rows = val.shape[2] // LANES
    half = chunk_rows * chunks

    @pl.when(step == 0)
    def _():
        skip_s[...] = jnp.zeros_like(skip_s)

    @pl.when(step < chunks)
    def _():
        for b in range(seqs):
            total = skip_s[...]
            for a in range(chunk_rows):
                lanes = slice(LANES * a, LANES * a + LANES)
                mixed = gin[b, :, lanes].astype(F32) * val[b, :, lanes].astype(F32)
                inner = cot[b, :, lanes].astype(F32) * gout[b, :, lanes].astype(F32)
                rows = pl.ds((step * chunk_rows + a) * (chans + 1), chans)
                mix_s[b, rows, :] = mixed
                grad_s[b, rows, :] = inner
                total = total + mixed * inner
            skip_s[...] = total

    @pl.when(step == chunks - 1)
    def _():
        per_row = jnp.sum(skip_s[...], axis=1, keepdims=True)
        lane = lax.broadcasted_iota(jnp.int32, (chans, LANES), 1)
        row = lax.broadcasted_iota(jnp.int32, (chans, LANES), 0)
        mine = lane == row + base_ref[0]
        spread = jnp.sum(jnp.where(mine, per_row, 0.0), axis=0, keepdims=True)
        top = lax.broadcasted_iota(jnp.int32, (8, LANES), 0) == 0
        skip_out[...] = jnp.where(top, spread, 0.0)

    @pl.when(step >= chunks)
    def _():
        pair = step - chunks
        tabs = (first, ahead, cos_t, sin_t)

        def job(number):
            b, inner = number // 2, number % 2 == 1
            source, target = (grad_s, fg_out) if inner else (mix_s, fm_out)
            r_ref, h_ref = r_s.at[number], h_s.at[number]

            def rows():
                parts = [
                    source[b, pl.ds(2 * pair + c, half, stride=chans + 1), :] for c in range(2)
                ]
                forward_rows(jnp.concatenate(parts, axis=1).astype(LOW), tabs, r_ref)

            def twist():
                forward_twist(tabs, r_ref, h_ref)

            def columns():
                f_s[number] = forward_columns(tabs, h_ref)
                target[b, 0] = f_s[number].astype(LOW)

            return rows, twist, columns

        staggered([job(number) for number in range(2 * seqs)])
        for g in range(half // 8 + 1):
            rows = slice(16 * g, 16 * g + 16)
            cross_re = cross_im = None
            for b in range(seqs):
                m_re, m_im = f_s[2 * b, rows, :LANES], f_s[2 * b, rows, LANES:]
                g_re, g_im = f_s[2 * b + 1, rows, :LANES], f_s[2 * b + 1, rows, LANES:]
                c_re = m_re * g_re + m_im * g_im
                c_im = m_re * g_im - m_im * g_re
                cross_re = c_re if b == 0 else cross_re + c_re
                cross_im = c_im if b == 0 else cross_im + c_im
            cross_s[rows, :LANES] = cross_re.astype(LOW)
            cross_s[rows, LANES:] = cross_im.astype(LOW)
        y = inverse_pair(cross_s, (back, last, cos_t, sin_t), b_s, t_s)
        members, _, each, _ = grad_out.shape
        for c in range(2):
            lanes = slice(LANES * c, LANES * c + LANES)
            grad_out[:, c] = y[:, lanes].reshape(members, each, LANES)


def norm_kernel(base_ref, raw, grads, after, grad_out, lines_out, *, length):
    step = pl.program_id(0)
    blocks, channels, rows_each, _ = raw.shape
    half = blocks * rows_each
    lane = lax.broadcasted_iota(jnp.int32, (8, LANES), 1)
    line = lax.broadcasted_iota(jnp.int32, (8, LANES), 0)
    position = (
        lax.broadcasted_iota(jnp.int32, (half, LANES), 0) * LANES
        + lax.broadcasted_iota(jnp.int32, (half, LANES), 1)
    ).astype(F32) * (-1.0 / length)

    @pl.when(step == 0)
    def _():
        lines_out[...] = jnp.zeros_like(lines_out)

    total = lines_out[...]
    for c in range(channels):
        row, grad = raw[:, c].reshape(half, LANES), grads[:, c].reshape(half, LANES)
        square_rows, cross_rows = row * row, row * grad
        square = jnp.sum(square_rows, keepdims=True) + EPSILON
        inv = 1.0 / jnp.sqrt(square)
        coef = jnp.sum(cross_rows, keepdims=True) * (inv / square)
        rate = inv * jnp.sum(cross_rows * position, keepdims=True) - coef * jnp.sum(
            square_rows * position, keepdims=True
        )
        grad_out[:, c] = (grad * inv - row * coef).reshape(blocks, rows_each, LANES)
        mine = lane == base_ref[0] + channels * step + c
        for number, x in enumerate((inv, rate)):
            total = jnp.where(jnp.logical_and(mine, line == number), x, total)
    lines_out[...] = total


def kernel_kernel(raw, after, first, ahead, cos_t, sin_t, fk_out, r_s, h_s):
    blocks, channels, rows_each, _ = raw.shape
    half = blocks * rows_each
    tabs = (first, ahead, cos_t, sin_t)

    def job(number):
        def rows():
            parts = [raw[:, 2 * number + c].reshape(half, LANES) for c in range(2)]
            signal = jnp.concatenate(parts, axis=1).astype(LOW)
            forward_rows(signal, tabs, r_s.at[number])

        def twist():
            forward_twist(tabs, r_s.at[number], h_s.at[number])

        def columns():
            fk_out[number] = forward_columns(tabs, h_s.at[number]).astype(LOW)

        return rows, twist, columns

    staggered([job(number) for number in range(channels // 2)])


def output_kernel(
    base_ref, fm, fg, fk, val, gin, gout, cot, skip, lines, back, last, cos_t, sin_t, *rest,
    steps, chunks, chans,
):
    val_out, gin_out, gout_out, token, conv_s, corr_s, s_s, b_s, t_s = rest[-9:]
    step = pl.program_id(0)
    chunk_rows = val.shape[2] // LANES
    half = chunk_rows * chunks
    together = fk.shape[0]

    @pl.when(step < steps)
    def _():
        tabs = (back, last, cos_t, sin_t)

        height = 2 * (half + 8)

        def job(p):
            s_ref, b_ref, t_ref = s_s.at[p], b_s.at[p], t_s.at[p]

            def product():
                for g in range(half // 8 + 1):
                    rows = slice(16 * g, 16 * g + 16)
                    lower = slice(height + 16 * g, height + 16 * g + 16)
                    k_re, k_im = fk[p, rows, :LANES].astype(F32), fk[p, rows, LANES:].astype(F32)
                    re, im = fm[0, p, rows, :LANES].astype(F32), fm[0, p, rows, LANES:].astype(F32)
                    s_ref[rows, :LANES] = (re * k_re - im * k_im).astype(LOW)
                    s_ref[rows, LANES:] = (re * k_im + im * k_re).astype(LOW)
                    re, im = fg[0, p, rows, :LANES].astype(F32), fg[0, p, rows, LANES:].astype(F32)
                    s_ref[lower, :LANES] = (re * k_re + im * k_im).astype(LOW)
                    s_ref[lower, LANES:] = (im * k_re - re * k_im).astype(LOW)

            def columns():
                inverse_columns(s_ref, tabs, b_ref)

            def twist():
                for number in range(2):
                    inverse_twist(
                        tabs,
                        b_ref.at[height * number : height * number + height],
                        t_ref.at[:, 2 * LANES * number : 2 * LANES * number + 2 * LANES],
                    )

            def finish():
                y = inverse_rows(tabs, t_ref)
                for number, target in enumerate((conv_s, corr_s)):
                    for c in range(2):
                        channel = 2 * (step * together + p) + c
                        lanes = LANES * (2 * number + c)
                        target[pl.ds(channel, half, stride=chans + 1), :] = y[
                            :, lanes : lanes + LANES
                        ]

            return product, columns, twist, finish

        staggered([job(p) for p in range(together)])

    @pl.when(step >= steps)
    def _():
        chunk = step - steps
        token[...] = jnp.zeros_like(token)
        gain = jnp.broadcast_to(column(skip[...], chans), (chans, LANES))
        lane = lax.broadcasted_iota(jnp.int32, (chans, LANES), 1)
        row = lax.broadcasted_iota(jnp.int32, (chans, LANES), 0)
        inv = jnp.sum(
            jnp.where(lane == row + base_ref[0], lines[0:1, :], 0.0), axis=1, keepdims=True
        )
        inv = jnp.broadcast_to(inv, (chans, LANES))
        for a in range(chunk_rows):
            lanes = slice(LANES * a, LANES * a + LANES)
            rows = pl.ds((chunk * chunk_rows + a) * (chans + 1), chans)
            v = val[0, :, lanes].astype(F32)
            gi = gin[0, :, lanes].astype(F32)
            go = gout[0, :, lanes].astype(F32)
            co = cot[0, :, lanes].astype(F32)
            inner = inv * conv_s[rows, :] + gain * (gi * v)
            grad_mixed = inv * corr_s[rows, :] + gain * (co * go)
            gout_out[0, :, lanes] = (co * inner).astype(LOW)
            val_out[0, :, lanes] = (grad_mixed * gi).astype(LOW)
            gin_out[0, :, lanes] = (grad_mixed * v).astype(LOW)


INV_PI = 0.3183098861837907


def fit(function, powers, top):
    nodes = np.cos(np.pi * (np.arange(400) + 0.5) / 800) * top
    design = np.stack([nodes**p for p in powers], axis=1)
    return [float(x) for x in np.linalg.lstsq(design, function(nodes), rcond=None)[0]]


SINE = fit(lambda x: np.sin(x) - x, (3, 5, 7, 9), np.pi / 2 + 1e-3)


def poly(coefficients, r2):
    p = coefficients[-1]
    for c in coefficients[-2::-1]:
        p = c + r2 * p
    return r2 * p


def sine_poly(r, r2):
    return r + r * poly(SINE, r2)


def turn_fit(function, powers):
    nodes = np.cos(np.pi * (np.arange(400) + 0.5) / 800) * 0.5
    design = np.stack([nodes**p for p in powers], axis=1)
    values = function(2.0 * np.pi * nodes)
    return [float(x) for x in np.linalg.lstsq(design, values, rcond=None)[0]]


TURN_SINE = turn_fit(np.sin, range(1, 15, 2))
TURN_COSINE = turn_fit(np.cos, range(0, 16, 2))


def horner(coefficients, u):
    p = coefficients[-1]
    for c in coefficients[-2::-1]:
        p = c + u * p
    return p


def turned_by(z):
    turns = z * (0.5 * INV_PI)
    return turns - jnp.floor(turns + 0.5)


def sine(z):
    f = turned_by(z)
    return f * horner(TURN_SINE, f * f)


def sine_cosine(z):
    f = turned_by(z)
    u = f * f
    return f * horner(TURN_SINE, u), horner(TURN_COSINE, u)


def column(row, size):
    lane = lax.broadcasted_iota(jnp.int32, (size, size), 1)
    diagonal = lane == lax.broadcasted_iota(jnp.int32, (size, size), 0)
    return jnp.sum(jnp.where(diagonal, row, 0.0), axis=1, keepdims=True)


def split(x):
    high = x.astype(LOW)
    return high, (x - high.astype(F32)).astype(LOW)


def triple_dot(weight, x):
    w_high, w_low = split(weight)
    x_high, x_low = split(x)
    wide = jnp.concatenate([w_high, w_high, w_low], axis=1)
    tall = jnp.concatenate([x_high, x_low, x_high], axis=0)
    return jnp.dot(wide, tall, preferred_element_type=F32)


def decay_tables(rates, start, channels, length):
    rate = column(rates, channels) * (-1.0 / length)
    lane = lax.broadcasted_iota(jnp.int32, (channels, LANES), 1)
    fine = jnp.exp(rate * lane.astype(F32))
    coarse = jnp.exp(rate * (start + LANES * lane).astype(F32))
    return fine, coarse


def features(start, freq, shift, width, length):
    rows = freq.shape[0]
    position = start + lax.broadcasted_iota(jnp.int32, (rows, width), 1)
    freq_w = jnp.concatenate([freq[...]] * (width // LANES), axis=1)
    shift_w = jnp.concatenate([shift[...]] * (width // LANES), axis=1)
    quarter = length // 4
    phase = position * freq_w + shift_w
    sign = (1 - ((phase >> int(math.log2(length // 2))) & 1) * 2).astype(F32)
    angle = ((phase & (length // 2 - 1)) - quarter).astype(F32) * (2.0 * math.pi / length)
    wave = sign * sine_poly(angle, angle * angle)
    linear = lax.broadcasted_iota(jnp.int32, (rows, width), 0) == 0
    return jnp.where(linear, position.astype(F32) * (1.0 / length), wave)


def widen(w_in, w_in_t):
    w_in[...] = jnp.zeros_like(w_in)
    w_in[:, : w_in_t.shape[0]] = w_in_t[...].T


def filter_kernel(
    start_ref, freq, shift, w_in_t, b_in, w_mid, b_mid, w_out_t, rates,
    raw_out, w_in, w_out, *, length,
):
    width = raw_out.shape[1] * LANES
    order = w_mid.shape[1]
    channels = w_out_t.shape[1]

    @pl.when(pl.program_id(0) == 0)
    def _():
        widen(w_in, w_in_t)
        w_out[...] = w_out_t[...].T

    start = start_ref[3] + pl.program_id(0) * width
    hidden = features(start, freq, shift, width, length)
    weights = ((w_in[...], b_in[...]), (w_mid[0], b_mid[0:1, :]), (w_mid[1], b_mid[1:2, :]))
    for weight, bias in weights:
        hidden = sine(triple_dot(weight, hidden) + column(bias, order))
    shaped = triple_dot(w_out[...], hidden)
    fine, coarse = decay_tables(rates[...], start, channels, length)
    for a in range(width // LANES):
        decay = fine * coarse[:, a : a + 1]
        raw_out[:, a, :] = shaped[:, LANES * a : LANES * a + LANES] * decay


def activation_kernel(
    start_ref, freq, shift, w_in_t, b_in, w_mid, b_mid, after,
    feat_out, act_out, cos_out, w_in, *, length,
):
    width = feat_out.shape[1]
    order = w_mid.shape[1]

    @pl.when(pl.program_id(0) == 0)
    def _():
        widen(w_in, w_in_t)

    start = start_ref[3] + pl.program_id(0) * width
    hidden = features(start, freq, shift, width, length)
    feat_out[...] = hidden.astype(LOW)
    weights = ((w_in[...], b_in[...]), (w_mid[0], b_mid[0:1, :]), (w_mid[1], b_mid[1:2, :]))
    for number, (weight, bias) in enumerate(weights):
        z = triple_dot(weight, hidden) + column(bias, order)
        hidden, cosine = sine_cosine(z)
        rows = slice(order * number, order * number + order)
        act_out[rows, :] = hidden.astype(LOW)
        cos_out[rows, :] = cosine.astype(LOW)


def double_dot(weight, x):
    wide = jnp.concatenate(split(weight), axis=1)
    return jnp.dot(wide, jnp.concatenate([x, x], axis=0), preferred_element_type=F32)


def nt_dot(x, y):
    return lax.dot_general(x, y, (((1,), (1,)), ((), ())), preferred_element_type=F32)


def filter_grad_kernel(
    start_ref, grad, feat, act, cosines, w_mid, w_out_t, rates, lines, skip_row, token,
    keep, give, d_out, d_mid, d_in, d_bias, packed, *, length,
):
    step = pl.program_id(0)
    width = feat.shape[1]
    order = w_mid.shape[1]
    channels = w_out_t.shape[1]
    start = start_ref[3] + step * width

    @pl.when(step == 0)
    def _():
        for ref in (d_out, d_mid, d_in, d_bias):
            ref[...] = jnp.zeros_like(ref)

    fine, coarse = decay_tables(rates[...], start, channels, length)
    parts = [grad[:, a, :] * (fine * coarse[:, a : a + 1]) for a in range(width // LANES)]
    d_shaped = jnp.concatenate(parts, axis=1)

    def part(ref, number):
        return ref[order * number : order * number + order, :]

    def bias_sum(x, number):
        total = x[:, :LANES]
        for a in range(1, width // LANES):
            total = total + x[:, LANES * a : LANES * a + LANES]
        d_bias[number] = d_bias[number] + total

    low = d_shaped.astype(LOW)
    d_out[...] = d_out[...] + nt_dot(low, part(act, 2))
    dz = double_dot(w_out_t[...], low) * part(cosines, 2).astype(F32)
    bias_sum(dz, 2)
    low = dz.astype(LOW)
    d_mid[1] = d_mid[1] + nt_dot(low, part(act, 1))
    dz = double_dot(w_mid[1].T, low) * part(cosines, 1).astype(F32)
    bias_sum(dz, 1)
    low = dz.astype(LOW)
    d_mid[0] = d_mid[0] + nt_dot(low, part(act, 0))
    dz = double_dot(w_mid[0].T, low) * part(cosines, 0).astype(F32)
    bias_sum(dz, 0)
    d_in[...] = d_in[...] + nt_dot(dz.astype(LOW), feat[...])

    @pl.when(step == pl.num_programs(0) - 1)
    def _():
        packed[...] = jnp.zeros_like(packed)
        packed[:channels, :order] = d_out[...]
        packed[:order, order : 2 * order] = d_mid[0]
        packed[order : 2 * order, order : 2 * order] = d_mid[1]
        base = channels
        features = d_in.shape[1]
        packed[base : base + order, :features] = d_in[...]
        spot = lax.broadcasted_iota(jnp.int32, (order, LANES), 1)
        current = packed[base : base + order, :]
        for number in range(3):
            total = jnp.sum(d_bias[number], axis=1, keepdims=True)
            current = jnp.where(spot == features + number, total, current)
        packed[base : base + order, :] = current
        base += order
        packed[base : base + 1, :] = lines[1:2, :]
        packed[base + 1 : base + 2, :] = skip_row[0:1, :]
        size = keep.shape[0]
        bit = start_ref[2]
        keep[...] = packed[pl.ds(pl.multiple_of(bit * size, 8), size), :]
        give[...] = packed[pl.ds(pl.multiple_of((1 - bit) * size, 8), size), :]


def unpack_kernel(
    base_ref, own, other, w_in_t, b_in, w_mid, b_mid, w_out_t, rate, skip, whole,
    *, scale, features,
):
    size = own.shape[0]
    bit = base_ref[2]
    whole[pl.ds(pl.multiple_of(bit * size, 8), size), :] = own[...] * scale
    whole[pl.ds(pl.multiple_of((1 - bit) * size, 8), size), :] = other[...] * scale
    order, channels = w_out_t.shape
    w_out_t[...] = whole[:channels, :].T[:order, :]
    mid = whole[: 2 * order, order : 2 * order]
    w_mid[0] = mid[:order]
    w_mid[1] = mid[order:]
    base = channels
    block = whole[base : base + order, :]
    w_in_t[...] = block.T[: w_in_t.shape[0], :]
    lane = lax.broadcasted_iota(jnp.int32, (order, LANES), 1)
    row = lax.broadcasted_iota(jnp.int32, (order, LANES), 0)

    def as_row(number):
        values = jnp.sum(jnp.where(lane == features + number, block, 0.0), axis=1, keepdims=True)
        return jnp.sum(jnp.where(lane == row, values, 0.0), axis=0, keepdims=True)[:, :order]

    b_in[...] = as_row(0)
    b_mid[0:1, :] = as_row(1)
    b_mid[1:2, :] = as_row(2)
    base += order
    rate[...] = whole[base : base + 1, :channels]
    chans = skip.shape[1]
    skips = whole[base + 1 : base + 2, :]
    lane = lax.broadcasted_iota(jnp.int32, (chans, LANES), 1)
    row = lax.broadcasted_iota(jnp.int32, (chans, LANES), 0)
    values = jnp.sum(jnp.where(lane == row + base_ref[0], skips, 0.0), axis=1, keepdims=True)
    skip[...] = jnp.sum(jnp.where(lane == row, values, 0.0), axis=0, keepdims=True)[:, :chans]


def const_spec(array):
    zeros = (0,) * len(array.shape)
    return pl.BlockSpec(array.shape, lambda i: zeros)


SCALAR = pl.BlockSpec(memory_space=pltpu.SMEM)


def vmem(shape, dtype=F32):
    return pltpu.VMEM(shape, dtype)


def shape(dims, dtype=F32):
    return jax.ShapeDtypeStruct(dims, dtype)


def exchange(x, axis, bit):
    size = lax.axis_size(axis)
    return lax.ppermute(x, axis, [(s, s ^ bit) for s in range(size)])


def fan_sum(x, axis, step):
    others = [exchange(x, axis, bit) for bit in range(step, lax.axis_size(axis), step)]
    return functools.reduce(jnp.add, others, x)


def local(
    value, gate_in, gate_out, cotangent, skip_gain,
    weight_in, bias_in, weight_mid, bias_mid, weight_out, decay_rate,
):
    seqs, chans, length = value.shape
    channels, order = weight_out.shape
    chan_count = lax.axis_size("chan")
    seq_count = lax.axis_size("seq")
    block = length // chan_count
    block_rows = block // LANES
    half = length // LANES
    pairs = chans // 2
    spec_rows = 2 * (half + 8)
    chunks = 4
    member = lax.axis_index("chan").astype(jnp.int32)
    base = jnp.stack([member * chans, member, member % 2, member * block])
    first, ahead, back, last, cos_t, sin_t = [jnp.asarray(t) for t in dft_tables(length)]
    feature_rows = 48
    bands = (weight_in.shape[1] - 1) // 2
    freq, shift = [jnp.asarray(t) for t in feature_tables(length, bands, feature_rows)]

    width = min(2048, block)
    steps = block // width
    rates = decay_rate.reshape(1, channels)
    w_out_t = weight_out.T
    w_in_t = weight_in.T
    weights = (w_in_t, bias_in.reshape(1, order), weight_mid, bias_mid)
    operands = (freq, shift) + weights
    raw_block = pl.pallas_call(
        functools.partial(filter_kernel, length=length),
        grid=(steps,),
        in_specs=[SCALAR] + [const_spec(x) for x in operands + (w_out_t, rates)],
        out_specs=pl.BlockSpec((channels, width // LANES, LANES), lambda i: (0, i, 0)),
        out_shape=shape((channels, block_rows, LANES)),
        scratch_shapes=[vmem((order, feature_rows)), vmem((channels, order))],
        name="filter_rows",
    )(base, *operands, w_out_t, rates)
    raw = lax.all_to_all(
        raw_block.reshape(chan_count, chans, block_rows, LANES),
        "chan", split_axis=0, concat_axis=0, tiled=True,
    )

    chunk = length // chunks
    tables = (first, ahead, back, last, cos_t, sin_t)
    early = lambda i: (0, 0, jnp.minimum(i, chunks - 1))
    late = lambda i: (0, jnp.maximum(i - chunks, 0), 0, 0)
    piece = lambda i: (0, jnp.maximum(i - chunks, 0), 0, 0)
    fm, fg, skip_row, grad_kernel = pl.pallas_call(
        functools.partial(
            spectra_kernel, chunks=chunks, seqs=seqs, chans=chans
        ),
        grid=(chunks + pairs,),
        in_specs=[SCALAR]
        + [pl.BlockSpec((seqs, chans, chunk), early)] * 4
        + [const_spec(x) for x in tables],
        out_specs=[
            pl.BlockSpec((seqs, 1, spec_rows, 2 * LANES), late),
            pl.BlockSpec((seqs, 1, spec_rows, 2 * LANES), late),
            pl.BlockSpec((8, LANES), lambda i: (0, 0)),
        ]
        + [pl.BlockSpec((chan_count, 2, block_rows, LANES), piece)],
        out_shape=[
            shape((seqs, pairs, spec_rows, 2 * LANES), LOW),
            shape((seqs, pairs, spec_rows, 2 * LANES), LOW),
            shape((8, LANES)),
        ]
        + [shape((chan_count, chans, block_rows, LANES))],
        scratch_shapes=[
            vmem((seqs, half * (chans + 1) + 16, LANES)),
            vmem((seqs, half * (chans + 1) + 16, LANES)),
            vmem((chans, LANES)),
            vmem((2 * seqs, 2 * half, 2 * LANES)),
            vmem((2 * seqs, spec_rows, 2 * LANES), LOW),
            vmem((2 * seqs, spec_rows, 2 * LANES)),
            vmem((spec_rows, 2 * LANES), LOW),
            vmem((spec_rows, 2 * LANES)),
            vmem((2 * half, 2 * LANES), LOW),
        ],
        name="spectra",
    )(base, value, gate_in, gate_out, cotangent, *tables)

    feats, acts, cosines = pl.pallas_call(
        functools.partial(activation_kernel, length=length),
        grid=(steps,),
        in_specs=[SCALAR] + [const_spec(x) for x in operands] + [pl.BlockSpec(memory_space=pl.ANY)],
        out_specs=[
            pl.BlockSpec((feature_rows, width), lambda i: (0, i)),
            pl.BlockSpec((3 * order, width), lambda i: (0, i)),
            pl.BlockSpec((3 * order, width), lambda i: (0, i)),
        ],
        out_shape=[
            shape((feature_rows, block), LOW),
            shape((3 * order, block), LOW),
            shape((3 * order, block), LOW),
        ],
        scratch_shapes=[vmem((order, feature_rows))],
        name="activations",
    )(base, *operands, skip_row)

    together = 4 if pairs % 4 == 0 else 1
    group = 2 * together
    many = 8 if chans % 8 == 0 else 2
    block_spec = lambda n: pl.BlockSpec((chan_count, n, block_rows, LANES), lambda i: (0, i, 0, 0))
    grad_raw, lines = pl.pallas_call(
        functools.partial(norm_kernel, length=length),
        grid=(chans // many,),
        in_specs=[SCALAR, block_spec(many), block_spec(many), pl.BlockSpec(memory_space=pl.ANY)],
        out_specs=[block_spec(many), pl.BlockSpec((8, LANES), lambda i: (0, 0))],
        out_shape=[shape((chan_count, chans, block_rows, LANES)), shape((8, LANES))],
        name="normalization",
    )(base, raw, grad_kernel, feats)
    taken = lax.all_to_all(grad_raw, "chan", split_axis=0, concat_axis=0, tiled=True)
    ahead_tabs = (first, ahead, cos_t, sin_t)
    fk = pl.pallas_call(
        kernel_kernel,
        grid=(pairs // together,),
        in_specs=[block_spec(group), pl.BlockSpec(memory_space=pl.ANY)]
        + [const_spec(x) for x in ahead_tabs],
        out_specs=pl.BlockSpec((together, spec_rows, 2 * LANES), lambda i: (i, 0, 0)),
        out_shape=shape((pairs, spec_rows, 2 * LANES), LOW),
        scratch_shapes=[
            vmem((together, 2 * half, 2 * LANES)),
            vmem((together, spec_rows, 2 * LANES), LOW),
        ],
        name="filter_spectrum",
    )(raw, lines, *ahead_tabs)

    back_tabs = (back, last, cos_t, sin_t)
    skip_line = skip_gain.reshape(1, chans)
    anywhere = pl.BlockSpec(memory_space=pl.ANY)
    out_steps = pairs // together

    out_chunks = 2

    def outputs(b, after, held):
        early4 = lambda i: (b, jnp.minimum(i, out_steps - 1), 0, 0)
        early3 = lambda i: (jnp.minimum(i, out_steps - 1), 0, 0)
        late3 = lambda i: (b, 0, jnp.maximum(i - out_steps, 0))
        signal_spec = pl.BlockSpec((1, chans, length // out_chunks), late3)
        wide_spec = pl.BlockSpec((1, together, spec_rows, 2 * LANES), early4)
        operands = (
            base, fm, fg, fk, value, gate_in, gate_out, cotangent, skip_line, lines,
        ) + back_tabs
        extras = tuple(after) + tuple(held)
        return pl.pallas_call(
            functools.partial(output_kernel, steps=out_steps, chunks=out_chunks, chans=chans),
            grid=(out_steps + out_chunks,),
            in_specs=[SCALAR, wide_spec, wide_spec]
            + [pl.BlockSpec((together, spec_rows, 2 * LANES), early3)]
            + [signal_spec] * 4
            + [const_spec(x) for x in (skip_line, lines) + back_tabs]
            + [anywhere] * len(extras),
            out_specs=[signal_spec] * 3 + [pl.BlockSpec((8, LANES), lambda i: (0, 0))],
            out_shape=[shape((seqs, chans, length), LOW)] * 3 + [shape((8, LANES))],
            input_output_aliases={
                len(operands) + len(after) + n: n for n in range(len(held))
            },
            scratch_shapes=[
                vmem((half * (chans + 1) + 16, LANES)),
                vmem((half * (chans + 1) + 16, LANES)),
                vmem((together, 2 * spec_rows, 2 * LANES), LOW),
                vmem((together, 2 * spec_rows, 2 * LANES)),
                vmem((together, 2 * half, 4 * LANES), LOW),
            ],
            name="outputs",
        )(*operands, *extras)

    held, token = (), lines
    for b in range(seqs):
        *held, token = outputs(b, (), held)

    packed_rows = -(-(channels + order + 2) // 16) * 16
    wide_spec = lambda rows: pl.BlockSpec((rows, width // LANES, LANES), lambda i: (0, i, 0))
    keep, give = pl.pallas_call(
        functools.partial(filter_grad_kernel, length=length),
        grid=(steps,),
        in_specs=[
            SCALAR,
            wide_spec(channels),
            pl.BlockSpec((feature_rows, width), lambda i: (0, i)),
            pl.BlockSpec((3 * order, width), lambda i: (0, i)),
            pl.BlockSpec((3 * order, width), lambda i: (0, i)),
        ]
        + [const_spec(x) for x in (weight_mid, w_out_t, rates, lines, skip_row)]
        + [anywhere],
        out_specs=[pl.BlockSpec((packed_rows // 2, LANES), lambda i: (0, 0))] * 2,
        out_shape=[shape((packed_rows // 2, LANES))] * 2,
        scratch_shapes=[
            vmem((channels, order)),
            vmem((2, order, order)),
            vmem((order, feature_rows)),
            vmem((3, order, LANES)),
            vmem((packed_rows, LANES)),
        ],
        name="filter_gradients",
    )(
        base, taken.reshape(channels, block_rows, LANES), feats, acts, cosines, weight_mid,
        w_out_t, rates, lines, skip_row, token,
    )
    grad_val, grad_gin, grad_gout = held

    own = fan_sum(keep + exchange(give, "chan", 1), "chan", 2)
    own = fan_sum(own, "seq", 1)
    other = exchange(own, "chan", 1)
    factor = 1.0 / math.sqrt(seqs * seq_count * length)
    d_in_t, d_bin, d_mid, d_bmid, d_out_t, d_rate, d_skip = pl.pallas_call(
        functools.partial(unpack_kernel, scale=factor, features=feature_rows),
        in_specs=[SCALAR, pl.BlockSpec(), pl.BlockSpec()],
        out_shape=[
            shape(weight_in.shape[::-1]),
            shape((1, order)),
            shape(weight_mid.shape),
            shape(bias_mid.shape),
            shape(weight_out.shape[::-1]),
            shape((1, channels)),
            shape((1, chans)),
        ],
        scratch_shapes=[vmem((packed_rows, LANES))],
        name="unpack",
    )(base, own, other)
    return (
        grad_val, grad_gin, grad_gout, d_skip[0],
        d_in_t.T, d_bin[0], d_mid, d_bmid, d_out_t.T, d_rate[0],
    )


def solution(mesh):
    large = P("seq", "chan", None)
    return jax.shard_map(
        local,
        mesh=mesh,
        in_specs=(large,) * 4 + (P("chan"),) + (P(),) * 6,
        out_specs=(large,) * 3 + (P("chan"),) + (P(),) * 6,
        check_vma=False,
    )
```
